512 devices in a mesh: rec: 8 (over x, y_hi), row: 4 (over y_lo), col: 16 (over z, core).
Axes of the slice: x: 4, y: 8 (y_hi: 2, y_lo: 4; y = y_hi * 4 + y_lo), z: 8, core: 2. Of those that a mesh axis runs over, the one named last changes fastest.
Arguments:
- local_derivs: bfloat16 [1024, 256, 128], P(('rec', 'row', 'col')), may hold values from -6 to 6
- global_derivs: bfloat16 [1024, 256, 384], P(('rec', 'row', 'col')), may hold values from -64 to 64
- weights: float32 [1024, 256], P(('rec', 'row', 'col')), may hold values from 0.25 to 4
- first_block: int32 [1024], P(('rec', 'row', 'col')), may hold values from 0 to 6
- bundle_count: int32 [512], P(('rec', 'row', 'col')), may hold values from 1 to 2
- trailing_block: float32 [8192, 8192], P(('rec', 'row'), 'col'), may hold values from -6 to 6
Outputs:
- updated: float32 [8192, 8192], P(('rec', 'row'), 'col')
The draws below stay inside these ranges and needn't reach their ends.
All inputs are finite; a program needn't handle non-finite values.
Results may differ from the reference program's by a relative error of at most 0.0094.
Values may be sent and summed in bfloat16 or wider, within the bound.
A program may use at most 64 MiB of HBM per device.

```python
import math
import jax
import jax.numpy as jnp
from jax import lax

BLK = 128
LOCAL = 128
PBLK = 8
ROWS = 256
NBD = 2
TRAIL = 8192
BUNDLES = 1024
N_REC = 8
N_ROW = 4
N_COL = 16
DEVICES = 512


def draw_global_derivs(key, part):
    base_key = jax.random.fold_in(key, 7101)
    noise_key = jax.random.fold_in(key, 7102)
    scale_key = jax.random.fold_in(key, 7103)
    full_shape = (BUNDLES, ROWS, 3 * BLK)
    base = 1.3 * jax.random.normal(base_key, full_shape, jnp.float32)
    fresh = 1.3 * jax.random.normal(noise_key, (BUNDLES, ROWS, BLK), jnp.float32)
    first_part = base[:, :, :BLK]
    second_part = 0.9 * first_part + 0.44 * fresh
    trail_part = base[:, :, 2 * BLK:]
    upper = jnp.float32(math.log(16.0))
    spread = jax.random.uniform(scale_key, (BLK,), jnp.float32, 0.0, 1.0) * upper
    scales = 16.0 * jnp.exp(spread - jnp.max(spread))
    scales = jnp.maximum(scales, 1.0)
    first_part = jnp.clip(first_part, -4.0, 4.0) * scales
    second_part = jnp.clip(second_part, -4.0, 4.0) * scales
    trail_part = jnp.clip(trail_part, -4.0, 4.0)
    whole = jnp.concatenate([first_part, second_part, trail_part], axis=2)
    return whole.astype(jnp.bfloat16)


def plant(array, rng, least, largest):
    longest = array.shape.index(max(array.shape))
    spots = []
    for shift in (0, 1):
        where = [jax.random.randint(jax.random.fold_in(rng, axis), (), 0, length) for axis, length in enumerate(array.shape)]
        where[longest] = (where[longest] + shift) % array.shape[longest]
        spots.append(tuple(where))
    return array.at[spots[0]].set(least).at[spots[1]].set(largest)


def level_of(rng, extent, cuts, low, largest):
    gain, own = 1.0, jax.random.fold_in(rng, 6)
    for dim, blocks in cuts:
        steps = jnp.exp(jax.random.uniform(jax.random.fold_in(own, dim), (blocks,), jnp.float32, low / len(cuts), largest / len(cuts)))
        gain = gain * jnp.repeat(steps, extent[dim] // blocks).reshape([-1 if axis == dim else 1 for axis in range(len(extent))])
    return gain


def normal_values(stream_key, shape, deviation, bound, cuts=(), kind=jnp.bfloat16):
    array = jax.random.normal(stream_key, shape, jnp.float32) * deviation
    if len(cuts) > 0:
        array = level_of(stream_key, shape, cuts, -0.22, 0.18) * array
    return jnp.clip(array, min=-bound, max=bound).astype(kind)


def setup_inputs(seed: int = 0) -> dict:
    key_list = jax.random.split(jax.random.key(seed), 7)
    local_derivs = normal_values(key_list[0], (BUNDLES, ROWS, LOCAL), 1.0, 6.0, ((0, 512),))
    global_derivs = draw_global_derivs(jax.random.fold_in(key_list[6], 71), 0)
    weights = jnp.clip(jnp.exp(math.log(4.0) - 2.7725887 * jax.random.uniform(key_list[2], (BUNDLES, ROWS), jnp.float32) ** level_of(key_list[2], (BUNDLES, ROWS), ((0, 512),), -0.2, 0.2)), 0.25, 4.0)
    first_block = plant(jax.random.randint(key_list[3], (BUNDLES,), 0, PBLK - 1), jax.random.fold_in(key_list[3], 1), 0, (PBLK - 1) - 1).astype(jnp.int32)
    bundle_count = plant(jax.random.randint(key_list[4], (DEVICES,), 1, NBD + 1), jax.random.fold_in(key_list[4], 1), 1, NBD).astype(jnp.int32)
    trailing_block = normal_values(key_list[5], (TRAIL, TRAIL), 1.0, 6.0, ((0, 32), (1, 16)), jnp.float32)
    return dict(local_derivs=local_derivs, global_derivs=global_derivs, weights=weights, first_block=first_block, bundle_count=bundle_count, trailing_block=trailing_block)


HIGH = lax.Precision.HIGHEST

def invert_lower(factor):
    eye = jnp.eye(factor.shape[-1], dtype=factor.dtype)
    eye = jnp.broadcast_to(eye, factor.shape)
    return lax.linalg.triangular_solve(factor, eye, left_side=True, lower=True)

def bundle_terms(local_derivs, global_derivs, weights, first_block, live):
    root = jnp.sqrt(weights)[:, :, None]
    scaled_local = (root * local_derivs.astype(jnp.float32)).astype(jnp.bfloat16).astype(jnp.float32)
    scaled_global = (root * global_derivs.astype(jnp.float32)).astype(jnp.bfloat16).astype(jnp.float32)
    local_gram = jnp.einsum('nrl,nrm->nlm', scaled_local, scaled_local, precision=HIGH)
    cross_gram = jnp.einsum('nrg,nrl->ngl', scaled_global, scaled_local, precision=HIGH)
    panel_gram = jnp.einsum('nra,nrg->nag', scaled_global[:, :, :2 * BLK], scaled_global, precision=HIGH)
    local_inverse = invert_lower(jnp.linalg.cholesky(local_gram))
    whitened = jnp.einsum('nlm,ngm->nlg', local_inverse, cross_gram, precision=HIGH)
    reduced = panel_gram - jnp.einsum('nla,nlg->nag', whitened[:, :, :2 * BLK], whitened, precision=HIGH)
    reduced = reduced * live[:, None, None]
    marks = jnp.arange(PBLK, dtype=jnp.int32)
    first_hot = (first_block[:, None] == marks[None, :]).astype(jnp.float32)
    second_hot = (first_block[:, None] + 1 == marks[None, :]).astype(jnp.float32)
    diag_part = jnp.einsum('nk,nab->kab', first_hot, reduced[:, :BLK, :BLK], precision=HIGH)
    diag_part = diag_part + jnp.einsum('nk,nab->kab', second_hot, reduced[:, BLK:2 * BLK, BLK:2 * BLK], precision=HIGH)
    sub_part = jnp.einsum('nk,nab->kab', second_hot, reduced[:, BLK:2 * BLK, :BLK], precision=HIGH)
    panel_part = jnp.einsum('nk,nab->kab', first_hot, reduced[:, :BLK, 2 * BLK:], precision=HIGH)
    panel_part = panel_part + jnp.einsum('nk,nab->kab', second_hot, reduced[:, BLK:2 * BLK, 2 * BLK:], precision=HIGH)
    return (jnp.stack([diag_part, sub_part], axis=1), panel_part.reshape(PBLK * BLK, BLK))

def step_block(diag, sub, panel_rows, inv_prev, sol_prev):
    low = jnp.dot(sub, inv_prev.T, precision=HIGH)
    inverse = invert_lower(jnp.linalg.cholesky(diag - jnp.dot(low, low.T, precision=HIGH)))
    solved = jnp.dot(inverse, panel_rows - jnp.dot(low, sol_prev, precision=HIGH), precision=HIGH)
    return (inverse, solved)

def reference(local_derivs, global_derivs, weights, first_block, bundle_count, trailing_block):
    shards = N_REC * N_ROW * N_COL
    stretches = N_ROW * N_COL
    local_split = local_derivs.reshape(shards, NBD, ROWS, LOCAL)
    global_split = global_derivs.reshape(shards, NBD, ROWS, 3 * BLK)
    weight_split = weights.reshape(shards, NBD, ROWS)
    first_split = first_block.reshape(shards, NBD)

    def visit(carry, items):
        block_total, panel = carry
        loc, glo, wts, first, count, shard = items
        live = (jnp.arange(NBD, dtype=jnp.int32) < count).astype(jnp.float32)
        stacked, panel_part = bundle_terms(loc, glo, wts, first, live)
        column = (shard % stretches * BLK).astype(jnp.int32)
        current = lax.dynamic_slice_in_dim(panel, column, BLK, 1)
        panel = lax.dynamic_update_slice_in_dim(panel, current + panel_part, column, 1)
        return ((block_total + stacked, panel), None)
    start = (jnp.zeros((PBLK, 2, BLK, BLK), jnp.float32), jnp.zeros((PBLK * BLK, TRAIL), jnp.float32))
    items = (local_split, global_split, weight_split, first_split, bundle_count, jnp.arange(shards, dtype=jnp.int32))
    (blocks, panel), _ = lax.scan(visit, start, items)
    inv_prev = jnp.eye(BLK, dtype=jnp.float32)
    sol_prev = jnp.zeros((BLK, TRAIL), jnp.float32)
    pieces = []
    for index in range(PBLK):
        rows = panel[index * BLK:(index + 1) * BLK]
        inv_prev, sol_prev = step_block(blocks[index, 0], blocks[index, 1], rows, inv_prev, sol_prev)
        pieces.append(sol_prev)
    solved_low = jnp.concatenate(pieces, axis=0).astype(jnp.bfloat16)
    update = lax.dot_general(solved_low.astype(jnp.float32), solved_low.astype(jnp.float32), (((0,), (0,)), ((), ())), preferred_element_type=jnp.float32)
    return trailing_block - update
```

```python
import functools

import jax
import jax.numpy as jnp
from jax import lax
from jax.experimental import pallas as pl
from jax.experimental.pallas import tpu as pltpu
from jax.sharding import PartitionSpec as P

HIGH = lax.Precision.HIGHEST
MESH = pl.DeviceIdType.MESH
BLK = 128
PBLK = 8
HALF = BLK // 2
F32 = jnp.float32
BF16 = jnp.bfloat16


def recip(x):
    r = pl.reciprocal(x, approx=True)
    r = r * (2.0 - x * r)
    return r * (2.0 - x * r)


def lane(x, at):
    return jnp.broadcast_to(x[:, at : at + 1], x.shape)


def row(x, at):
    return jnp.broadcast_to(x[at : at + 1, :], x.shape)


def strip_sweep(strips, j, base, sub, lan):
    inside = (lan >= base) & (lan < base + 8)
    panel = strips[j]
    others = [o for o in range(len(strips)) if o != j]
    cols = [lane(panel, base + k) for k in range(8)]
    outer = [[lane(strips[o], base + k) for o in others] for k in range(8)]
    x = jnp.where(inside, jnp.where(lan - base == sub, -1.0, 0.0), panel)
    for i in range(0, 8, 2):
        c0, c1 = cols[i], cols[i + 1]
        a, b, c = row(c0, i), row(c0, i + 1), row(c1, i + 1)
        rd = recip(a * c - b * b)
        first, second = sub == i, sub == i + 1
        ra, rb, rc = a * rd, b * rd, c * rd

        def step(v):
            p, q = row(v, i), row(v, i + 1)
            u = rc * p - rb * q
            w = ra * q - rb * p
            return jnp.where(first, u, jnp.where(second, w, v - c0 * u - c1 * w))

        cols = [step(v) if k > i + 1 else v for k, v in enumerate(cols)]
        x = step(x)
    rows = [row(x, k) for k in range(8)]
    new = list(strips)
    for at, o in enumerate(others):
        acc = jnp.where(inside, 0.0, strips[o])
        for k in range(8):
            acc = acc - outer[k][at] * rows[k]
        new[o] = acc
    new[j] = x
    return new


def minus_inverse(mats, width=2):
    n = mats[0].shape[0]
    h = 8 * width
    sub = lax.broadcasted_iota(jnp.int32, (8, n), 0)
    lan = lax.broadcasted_iota(jnp.int32, (8, n), 1)
    wide = lax.broadcasted_iota(jnp.int32, (n, n), 1)
    for low in range(0, n, h):
        panels = [[a[low + 8 * s : low + 8 * s + 8, :] for s in range(width)] for a in mats]
        for s in range(width):
            panels = [strip_sweep(p, s, low + 8 * s, sub, lan) for p in panels]
        out = []
        for a, p in zip(mats, panels):
            w = jnp.concatenate(p, axis=0)
            above = [jnp.zeros((low, n), F32)] if low else []
            below = [jnp.zeros((n - low - h, n), F32)] if low + h < n else []
            pad = jnp.concatenate(above + [w] + below, axis=0)
            keep = jnp.where((wide >= low) & (wide < low + h), 0.0, a)
            new = keep - jnp.dot(a, pad, precision=HIGH, preferred_element_type=F32)
            parts = ([new[:low]] if low else []) + [w] + ([new[low + h :]] if low + h < n else [])
            out.append(jnp.concatenate(parts, axis=0))
        mats = out
    return mats


def dot(a, b):
    return jnp.dot(a, b, precision=HIGH, preferred_element_type=F32)


def dot_t(a, b):
    return lax.dot_general(a, b, (((1,), (1,)), ((), ())), precision=HIGH, preferred_element_type=F32)


def t_dot(a, b, precision=HIGH):
    return lax.dot_general(
        a, b, (((0,), (0,)), ((), ())), precision=precision, preferred_element_type=F32
    )


def bundle_kernel(first_ref, count_ref, loc_ref, glo_ref, wts_ref, t_ref, p_ref):
    slots = loc_ref.shape[0]
    rows = loc_ref.shape[1]
    grams, crosses, panels = [], [], []
    for b in range(slots):
        columns = []
        for part in range(rows // BLK):
            w = jnp.sqrt(wts_ref[b : b + 1, part * BLK : part * BLK + BLK])
            column = jnp.transpose(jnp.broadcast_to(w, (8, BLK)))[:, 0:1]
            columns.append(column)
        root = jnp.concatenate(columns, axis=0)
        sl = (root * loc_ref[b].astype(F32)).astype(BF16)
        sg = (root * glo_ref[b].astype(F32)).astype(BF16)
        grams.append(t_dot(sl, sl, None))
        crosses.append(t_dot(sl, sg, None))
        panels.append(t_dot(sg[:, : 2 * BLK], sg, None))
    minus = minus_inverse(grams)
    reduced = []
    for b in range(slots):
        live = (b < count_ref[0]).astype(F32)
        fitted = dot(minus[b], crosses[b])
        reduced.append((panels[b] + t_dot(crosses[b][:, : 2 * BLK], fitted)) * live)
    for k in range(PBLK):
        diag = jnp.zeros((BLK, BLK), F32)
        below = jnp.zeros((BLK, BLK), F32)
        rhs = jnp.zeros((BLK, BLK), F32)
        for b in range(slots):
            first = (first_ref[b] == k).astype(F32)
            second = (first_ref[b] + 1 == k).astype(F32)
            r = reduced[b]
            if k < PBLK - 1:
                diag = diag + first * r[:BLK, :BLK]
                rhs = rhs + first * r[:BLK, 2 * BLK :]
            if k > 0:
                diag = diag + second * r[BLK:, BLK : 2 * BLK]
                below = below + second * r[BLK:, :BLK]
                rhs = rhs + second * r[BLK:, 2 * BLK :]
        t_ref[0, k] = diag.astype(BF16)
        t_ref[1, k] = below.astype(BF16)
        p_ref[k] = rhs.astype(BF16)


def device(x, h, l, z, c):
    return {"rec": x * 2 + h, "row": l, "col": z * 2 + c}


def remote(src, dst, send_sem, recv_sem, to):
    return pltpu.make_async_remote_copy(
        src_ref=src,
        dst_ref=dst,
        send_sem=send_sem,
        recv_sem=recv_sem,
        device_id=to,
        device_id_type=MESH,
    )


def loop(low, high, step):
    def one(at, carry):
        step(at)
        return carry

    lax.fori_loop(low, high, one, 0)


def exchange_kernel(
    t_in, p_in, t_out, left, right,
    tc, ts, tz1, ty1, tz2, ty2, tx, half2, half3, px, pa, pp, py, pc,
    s_tc, r_tc, s_z1, r_z1, s_y1, r_y1, s_z2, r_z2, s_y2, r_y2, s_tx, r_tx,
    s_z3, r_z3, s_y3, r_y3, s_f, r_f, s_px, r_px, s_py, r_py,
    s_rg, r_rg, s_lg, r_lg, s_ry, r_ry, s_rx, r_rx, s_lz, r_lz, s_lc, r_lc,
):
    rec, l, col = lax.axis_index("rec"), lax.axis_index("row"), lax.axis_index("col")
    x, h, z, c = rec // 2, rec % 2, col // 2, col % 2
    y = h * 4 + l
    me = device(x, h, l, z, c)
    pair = device(x, h, l, z, 1 - c)
    partner = device(x, 1 - h, l, z, c)

    def at_z(i):
        return device(x, h, l, i, c)

    def at_y(i):
        return device(x, i // 4, i % 4, z, c)

    def at_x(i):
        return device(i, h, l, z, c)

    mine = 2 * x + h
    right_source = z // 2 == l
    left_source = y == z
    right_z, right_c, right_j = 2 * l + z // 4, (z % 4) // 2, 2 * (z % 2) + c
    right_home = (right_z == z) & (right_c == c)
    right_to = device(x, h, l, right_z, right_c)
    left_home = (l == x) & (z == y)
    left_to = device(l, z // 4, z % 4, z, c)

    barrier = pltpu.get_barrier_semaphore()

    def greet(to):
        pl.semaphore_signal(barrier, inc=1, device_id=to, device_id_type=MESH)

    greet(pair)
    loop(1, 8, lambda d: greet(at_z((z + d) % 8)))
    loop(1, 8, lambda d: greet(at_y((y + d) % 8)))
    loop(1, 4, lambda d: greet(at_x((x + d) % 4)))

    @pl.when(right_source)
    def _():
        for j in range(4):
            from_z, from_c = 4 * (z % 2) + 2 * c + j // 2, j % 2

            @pl.when((from_z != z) | (from_c != c))
            def _():
                greet(device(x, h, l, from_z, from_c))

    @pl.when(left_source)
    def _():
        for k in range(8):

            @pl.when((k != mine) | (l != x))
            def _():
                greet(device(k // 2, k % 2, x, z, c))

    away = jnp.where(right_home, 0, 1) + jnp.where(left_home, 0, 1)
    pl.semaphore_wait(barrier, 18 + away)

    copy_tc = remote(t_in.at[1 - c], tc, s_tc, r_tc, pair)
    copy_tc.start()

    def panel_x(d):
        to = (x + d) % 4
        return remote(p_in.at[pl.ds(2 * to, 2)], px.at[d], s_px.at[d], r_px.at[d], at_x(to))

    loop(1, 4, lambda d: panel_x(d).start())

    copy_tc.wait_recv()

    def pair_sum(i):
        ts[i] = (t_in[c, i].astype(F32) + tc[i].astype(F32)).astype(BF16)

    loop(0, 8, pair_sum)

    def send_z1(d):
        to = (z + d) % 8
        return remote(ts.at[to, pl.ds(0, HALF)], tz1.at[d], s_z1.at[d], r_z1.at[d], at_z(to))

    def send_y1(d):
        to = (y + d) % 8
        return remote(ts.at[to, pl.ds(HALF, HALF)], ty1.at[d], s_y1.at[d], r_y1.at[d], at_y(to))

    def start_1(d):
        send_z1(d).start()
        send_y1(d).start()

    loop(1, 8, start_1)

    for d in range(1, 4):
        panel_x(d).wait_recv()
    for hh in range(2):
        total = p_in[2 * x + hh].astype(F32)
        for d in range(1, 4):
            total = total + px[d, hh].astype(F32)
        pa[hh] = total
    pp[...] = pa[1 - h].astype(BF16)
    copy_py = remote(pp, py, s_py, r_py, partner)
    copy_py.start()

    def wait_1(d):
        send_z1(d).wait_recv()
        send_y1(d).wait_recv()

    loop(1, 8, wait_1)
    sum_z = ts[z, 0:HALF].astype(F32)
    sum_y = ts[y, HALF:BLK].astype(F32)
    for d in range(1, 8):
        sum_z = sum_z + tz1[d].astype(F32)
        sum_y = sum_y + ty1[d].astype(F32)
    half2[0] = sum_z.astype(BF16)
    half2[1] = sum_y.astype(BF16)

    def send_y2(d):
        to = (y + d) % 8
        return remote(half2.at[0], ty2.at[d], s_y2.at[d], r_y2.at[d], at_y(to))

    def send_z2(d):
        to = (z + d) % 8
        return remote(half2.at[1], tz2.at[d], s_z2.at[d], r_z2.at[d], at_z(to))

    def start_2(d):
        send_y2(d).start()
        send_z2(d).start()

    loop(1, 8, start_2)

    copy_py.wait_recv()
    piece = (pa[h] + py[...].astype(F32)).astype(BF16)
    pc[...] = piece
    copy_rg = remote(pc, right.at[mine, right_j], s_rg, r_rg.at[right_j], right_to)
    copy_lg = remote(pc, left.at[c, mine], s_lg, r_lg.at[mine], left_to)

    @pl.when(right_home)
    def _():
        right[mine, right_j] = piece

    @pl.when(jnp.logical_not(right_home))
    def _():
        copy_rg.start()

    @pl.when(left_home)
    def _():
        left[c, mine] = piece

    @pl.when(jnp.logical_not(left_home))
    def _():
        copy_lg.start()

    def wait_2(d):
        send_y2(d).wait_recv()
        send_z2(d).wait_recv()

    loop(1, 8, wait_2)
    sum_z = half2[0].astype(F32)
    sum_y = half2[1].astype(F32)
    for d in range(1, 8):
        sum_z = sum_z + ty2[d].astype(F32)
        sum_y = sum_y + tz2[d].astype(F32)
    half3[0] = sum_z
    half3[1] = sum_y

    def send_tx(d):
        return remote(half3, tx.at[d], s_tx.at[d], r_tx.at[d], at_x((x + d) % 4))

    loop(1, 4, lambda d: send_tx(d).start())
    loop(1, 4, lambda d: send_tx(d).wait_recv())
    sum_z, sum_y = half3[0], half3[1]
    for d in range(1, 4):
        sum_z = sum_z + tx[d, 0]
        sum_y = sum_y + tx[d, 1]
    t_out[c, z, 0:HALF] = sum_z
    t_out[c, y, HALF:BLK] = sum_y

    def upper(cc, i):
        return t_out.at[cc, i, pl.ds(0, HALF)]

    def lower(cc, i):
        return t_out.at[cc, i, pl.ds(HALF, HALF)]

    def send_z3(d):
        return remote(upper(c, z), upper(c, z), s_z3.at[d], r_z3.at[d], at_z((z + d) % 8))

    def send_y3(d):
        return remote(lower(c, y), lower(c, y), s_y3.at[d], r_y3.at[d], at_y((y + d) % 8))

    def got_z3(d):
        i = (z + 8 - d) % 8
        return remote(upper(c, i), upper(c, i), s_z3.at[d], r_z3.at[d], at_z(i))

    def got_y3(d):
        i = (y + 8 - d) % 8
        return remote(lower(c, i), lower(c, i), s_y3.at[d], r_y3.at[d], at_y(i))

    def across_z(cc, i):
        return remote(upper(cc, i), upper(cc, i), s_f.at[i], r_f.at[i], pair)

    def across_y(cc, i):
        return remote(lower(cc, i), lower(cc, i), s_f.at[8 + i], r_f.at[8 + i], pair)

    def start_3(d):
        send_z3(d).start()
        send_y3(d).start()

    loop(1, 8, start_3)
    across_z(c, z).start()
    across_y(c, y).start()

    def right_y(d):
        return remote(right.at[mine], right.at[mine], s_ry.at[d], r_ry.at[h], at_y((y + d) % 8))

    def left_z(d):
        return remote(left.at[c], left.at[c], s_lz.at[d], r_lz, at_z((z + d) % 8))

    @pl.when(right_source)
    def _():
        for j in range(4):
            from_z, from_c = 4 * (z % 2) + 2 * c + j // 2, j % 2

            @pl.when((from_z != z) | (from_c != c))
            def _():
                remote(pc, right.at[mine, j], s_rg, r_rg.at[j], device(x, h, l, from_z, from_c)).wait_recv()

        loop(1, 8, lambda d: right_y(d).start())

    @pl.when(left_source)
    def _():
        for k in range(8):

            @pl.when((k != mine) | (l != x))
            def _():
                remote(pc, left.at[c, k], s_lg, r_lg.at[k], device(k // 2, k % 2, x, z, c)).wait_recv()

        loop(1, 8, lambda d: left_z(d).start())

    def arrived_3(d):
        got_z3(d).wait_recv()
        across_z(c, (z + 8 - d) % 8).start()
        got_y3(d).wait_recv()
        across_y(c, (y + 8 - d) % 8).start()

    loop(1, 8, arrived_3)

    def right_x(hh, d):
        block = right.at[2 * x + hh]
        at = hh * 4 + d
        return remote(block, block, s_rx.at[at], r_rx.at[at], at_x((x + d) % 4))

    for hh in range(2):
        source = 4 * hh + z // 2

        @pl.when(y != source)
        def _():
            block = right.at[2 * x + hh]
            remote(block, block, s_ry.at[0], r_ry.at[hh], at_y(source)).wait_recv()

        loop(1, 4, lambda d: right_x(hh, d).start())

    @pl.when(y != z)
    def _():
        remote(left.at[c], left.at[c], s_lz.at[0], r_lz, at_z(y)).wait_recv()

    copy_lc = remote(left.at[c], left.at[c], s_lc, r_lc, pair)
    copy_lc.start()

    def across(i):
        across_z(1 - c, i).wait_recv()
        across_y(1 - c, i).wait_recv()

    loop(0, 8, across)
    remote(left.at[1 - c], left.at[1 - c], s_lc, r_lc, pair).wait_recv()
    for hh in range(2):

        def got_x(d):
            i = (x + 4 - d) % 4
            block = right.at[2 * i + hh]
            remote(block, block, s_rx.at[hh * 4 + d], r_rx.at[hh * 4 + d], at_x(i)).wait_recv()

        loop(1, 4, got_x)

    copy_tc.wait_send()
    copy_py.wait_send()
    copy_lc.wait_send()

    @pl.when(jnp.logical_not(right_home))
    def _():
        copy_rg.wait_send()

    @pl.when(jnp.logical_not(left_home))
    def _():
        copy_lg.wait_send()

    def sent_7(d):
        send_z1(d).wait_send()
        send_y1(d).wait_send()
        send_z2(d).wait_send()
        send_y2(d).wait_send()
        send_z3(d).wait_send()
        send_y3(d).wait_send()

    loop(1, 8, sent_7)

    def sent_3(d):
        panel_x(d).wait_send()
        send_tx(d).wait_send()
        right_x(0, d).wait_send()
        right_x(1, d).wait_send()

    loop(1, 4, sent_3)

    def sent_8(i):
        across_z(c, i).wait_send()
        across_y(c, i).wait_send()

    loop(0, 8, sent_8)

    @pl.when(right_source)
    def _():
        loop(1, 8, lambda d: right_y(d).wait_send())

    @pl.when(left_source)
    def _():
        loop(1, 8, lambda d: left_z(d).wait_send())


def eliminate_kernel(t_ref, left_ref, right_ref, trail_ref, out_ref, p_ref):
    for k in range(PBLK):
        for i in range(2):
            p_ref[k, :, i * BLK : i * BLK + BLK] = left_ref[i, k].astype(F32)
        for j in range(4):
            p_ref[k, :, (2 + j) * BLK : (3 + j) * BLK] = right_ref[k, j].astype(F32)
    diag = [t_ref[0, k] for k in range(PBLK)]
    below = [None] + [t_ref[1, k] for k in range(1, PBLK)]
    out_ref[...] = trail_ref[...]

    def couple(gain, source, target):
        p_ref[target] = p_ref[target] + dot(gain, p_ref[source])

    def finish(k, minus):
        solved = dot(minus, p_ref[k, :, 2 * BLK :])
        out_ref[...] = out_ref[...] + t_dot(p_ref[k, :, : 2 * BLK], solved)

    n0, n2, n5, n7 = minus_inverse([diag[0], diag[2], diag[5], diag[7]])
    g01 = dot(below[1], n0)
    g21 = t_dot(below[2], n2)
    g23 = dot(below[3], n2)
    g54 = t_dot(below[5], n5)
    g56 = dot(below[6], n5)
    g76 = t_dot(below[7], n7)
    d1 = diag[1] + dot_t(g01, below[1]) + dot(g21, below[2])
    d6 = diag[6] + dot_t(g56, below[6]) + dot(g76, below[7])
    d3 = diag[3] + dot_t(g23, below[3])
    d4 = diag[4] + dot(g54, below[5])
    f31 = dot(g23, below[2])
    f64 = dot(g56, below[5])
    couple(g01, 0, 1)
    couple(g21, 2, 1)
    couple(g23, 2, 3)
    couple(g54, 5, 4)
    couple(g56, 5, 6)
    couple(g76, 7, 6)
    n1, n6 = minus_inverse([d1, d6])
    g13 = dot(f31, n1)
    g64 = t_dot(f64, n6)
    d3 = d3 + dot_t(g13, f31)
    d4 = d4 + dot(g64, f64)
    couple(g13, 1, 3)
    couple(g64, 6, 4)
    (n3,) = minus_inverse([d3])
    g34 = dot(below[4], n3)
    d4 = d4 + dot_t(g34, below[4])
    couple(g34, 3, 4)
    (n4,) = minus_inverse([d4])
    for k, minus in enumerate((n0, n1, n2, n3, n4, n5, n6, n7)):
        finish(k, minus)


def body(local_derivs, global_derivs, weights, first_block, bundle_count, trailing_block):
    vmem = pl.BlockSpec(memory_space=pltpu.VMEM)
    smem = pl.BlockSpec(memory_space=pltpu.SMEM)
    block = (BLK, BLK)
    shape = jax.ShapeDtypeStruct
    tri, panel = pl.pallas_call(
        bundle_kernel,
        name="bundles",
        in_specs=[smem, smem, vmem, vmem, vmem],
        out_specs=[vmem, vmem],
        out_shape=[shape((2, PBLK) + block, BF16), shape((PBLK,) + block, BF16)],
    )(first_block, bundle_count, local_derivs, global_derivs, weights)
    dma = pltpu.SemaphoreType.DMA
    half = (HALF, BLK)
    sems = (
        [dma, dma]
        + [dma((8,))] * 8
        + [dma((4,))] * 2
        + [dma((8,))] * 4
        + [dma((16,))] * 2
        + [dma((4,))] * 2
        + [dma, dma]
        + [dma, dma((4,)), dma, dma((8,))]
        + [dma((8,)), dma((2,)), dma((8,)), dma((8,))]
        + [dma((8,)), dma, dma, dma]
    )
    tri, left, right = pl.pallas_call(
        exchange_kernel,
        name="exchange",
        in_specs=[vmem, vmem],
        out_specs=[vmem, vmem, vmem],
        out_shape=[
            shape((2, PBLK) + block, F32),
            shape((2, PBLK) + block, BF16),
            shape((PBLK, 4) + block, BF16),
        ],
        scratch_shapes=[
            pltpu.VMEM((PBLK,) + block, BF16),
            pltpu.VMEM((PBLK,) + block, BF16),
            pltpu.VMEM((8,) + half, BF16),
            pltpu.VMEM((8,) + half, BF16),
            pltpu.VMEM((8,) + half, BF16),
            pltpu.VMEM((8,) + half, BF16),
            pltpu.VMEM((4, 2) + half, F32),
            pltpu.VMEM((2,) + half, BF16),
            pltpu.VMEM((2,) + half, F32),
            pltpu.VMEM((4, 2) + block, BF16),
            pltpu.VMEM((2,) + block, F32),
            pltpu.VMEM(block, BF16),
            pltpu.VMEM(block, BF16),
            pltpu.VMEM(block, BF16),
        ]
        + sems,
        compiler_params=pltpu.CompilerParams(collective_id=0, has_side_effects=True),
    )(tri, panel)
    return pl.pallas_call(
        eliminate_kernel,
        name="eliminate",
        in_specs=[vmem] * 4,
        out_specs=vmem,
        out_shape=shape(trailing_block.shape, F32),
        scratch_shapes=[pltpu.VMEM((PBLK, BLK, 6 * BLK), F32)],
    )(tri, left, right, trailing_block)


def solution(mesh):
    return jax.shard_map(
        body,
        mesh=mesh,
        in_specs=(
            P(("rec", "row", "col"), None, None),
            P(("rec", "row", "col"), None, None),
            P(("rec", "row", "col"), None),
            P(("rec", "row", "col")),
            P(("rec", "row", "col")),
            P(("rec", "row"), "col"),
        ),
        out_specs=P(("rec", "row"), "col"),
        check_vma=False,
    )
```

```python
import functools

import jax
import jax.numpy as jnp
from jax import lax
from jax.experimental import pallas as pl
from jax.experimental.pallas import tpu as pltpu
from jax.sharding import PartitionSpec as P

HIGH = lax.Precision.HIGHEST
MESH = pl.DeviceIdType.MESH
BLK = 128
PBLK = 8
HALF = BLK // 2
STRIPS = 4
F32 = jnp.float32
BF16 = jnp.bfloat16


def recip(x):
    r = pl.reciprocal(x, approx=True)
    return r * (2.0 - x * r)


def row(v, i):
    return jnp.broadcast_to(v[..., i:i + 1, :], v.shape)


def tree(v):
    while v.shape[0] > 1:
        half = v.shape[0] // 2
        v = v[:half] + v[half:]
    return v[0]


def strip_sweep(strips, j, base, sub, lan):
    inside = (lan >= base) & (lan < base + 8)
    panel = strips[j]
    shape = panel.shape

    def columns(s):
        return [jnp.broadcast_to(s[:, :, base + k:base + k + 1], shape) for k in range(8)]

    others = [o for o in range(len(strips)) if o != j]
    state = columns(panel)
    outer = [columns(strips[o]) for o in others]
    state = jnp.stack(state + [jnp.where(inside, jnp.where(lan - base == sub, -1.0, 0.0), panel)])
    for i in range(0, 8, 2):
        c0, c1 = state[0], state[1]
        a, b, c = row(c0, i), row(c0, i + 1), row(c1, i + 1)
        rd = recip(a * c - b * b)
        v = state[2:]
        p, q = row(v, i), row(v, i + 1)
        u = (c * rd) * p - (b * rd) * q
        w = (a * rd) * q - (b * rd) * p
        state = jnp.where(sub == i, u, jnp.where(sub == i + 1, w, v - (c0 * u + c1 * w)))
    x = state[0]
    rows = jnp.stack([row(x, k) for k in range(8)])
    new = list(strips)
    for at, o in enumerate(others):
        new[o] = jnp.where(inside, 0.0, strips[o]) - tree(jnp.stack(outer[at]) * rows)
    new[j] = x
    return new


def minus_inverse(mats):
    n = mats[0].shape[0]
    h = 8 * STRIPS
    sub = lax.broadcasted_iota(jnp.int32, (8, n), 0)
    lan = lax.broadcasted_iota(jnp.int32, (8, n), 1)
    wide = lax.broadcasted_iota(jnp.int32, (n, n), 1)
    for low in range(0, n, h):
        strips = [jnp.stack([a[low + 8 * s:low + 8 * s + 8, :] for a in mats]) for s in range(STRIPS)]
        for s in range(STRIPS):
            strips = strip_sweep(strips, s, low + 8 * s, sub, lan)
        out = []
        for m, a in enumerate(mats):
            w = jnp.concatenate([s[m] for s in strips], axis=0)
            above = [jnp.zeros((low, n), F32)] if low else []
            below = [jnp.zeros((n - low - h, n), F32)] if low + h < n else []
            pad = jnp.concatenate(above + [w] + below, axis=0)
            keep = jnp.where((wide >= low) & (wide < low + h), 0.0, a)
            new = keep - jnp.dot(a, pad, precision=HIGH, preferred_element_type=F32)
            parts = ([new[:low]] if low else []) + [w] + ([new[low + h:]] if low + h < n else [])
            out.append(jnp.concatenate(parts, axis=0))
        mats = out
    return mats


def dot(a, b):
    return jnp.dot(a, b, precision=HIGH, preferred_element_type=F32)


def dot_t(a, b):
    return lax.dot_general(a, b, (((1,), (1,)), ((), ())), precision=HIGH, preferred_element_type=F32)


def t_dot(a, b, precision=HIGH):
    return lax.dot_general(
        a, b, (((0,), (0,)), ((), ())), precision=precision, preferred_element_type=F32
    )


def bundle_terms(first_ref, count_ref, loc_ref, glo_ref, wts_ref, t_ref, p_ref):
    slots = loc_ref.shape[0]
    rows = loc_ref.shape[1]
    grams, crosses, panels = [], [], []
    for b in range(slots):
        columns = []
        for part in range(rows // BLK):
            w = jnp.sqrt(wts_ref[b : b + 1, part * BLK : part * BLK + BLK])
            column = jnp.transpose(jnp.broadcast_to(w, (8, BLK)))[:, 0:1]
            columns.append(column)
        root = jnp.concatenate(columns, axis=0)
        sl = (root * loc_ref[b].astype(F32)).astype(BF16)
        sg = (root * glo_ref[b].astype(F32)).astype(BF16)
        grams.append(t_dot(sl, sl, None))
        crosses.append(t_dot(sl, sg, None))
        panels.append(t_dot(sg[:, : 2 * BLK], sg, None))
    minus = minus_inverse(grams)
    reduced = []
    for b in range(slots):
        live = (b < count_ref[0]).astype(F32)
        fitted = dot(minus[b], crosses[b])
        reduced.append((panels[b] + t_dot(crosses[b][:, : 2 * BLK], fitted)) * live)
    for k in range(PBLK):
        diag = jnp.zeros((BLK, BLK), F32)
        below = jnp.zeros((BLK, BLK), F32)
        rhs = jnp.zeros((BLK, BLK), F32)
        for b in range(slots):
            first = (first_ref[b] == k).astype(F32)
            second = (first_ref[b] + 1 == k).astype(F32)
            r = reduced[b]
            if k < PBLK - 1:
                diag = diag + first * r[:BLK, :BLK]
                rhs = rhs + first * r[:BLK, 2 * BLK :]
            if k > 0:
                diag = diag + second * r[BLK:, BLK : 2 * BLK]
                below = below + second * r[BLK:, :BLK]
                rhs = rhs + second * r[BLK:, 2 * BLK :]
        t_ref[0, k] = diag.astype(BF16)
        t_ref[1, k] = below.astype(BF16)
        p_ref[k] = rhs.astype(BF16)


def eliminate(t_ref, left_ref, right_ref, out_ref, p_ref, between, panel_ready):
    diag = [t_ref[0, k] for k in range(PBLK)]
    below = [None] + [t_ref[1, k] for k in range(1, PBLK)]

    def couple(gain, source, target):
        p_ref[target] = p_ref[target] + dot(gain, p_ref[source])

    n0, n2, n5, n7 = minus_inverse([diag[0], diag[2], diag[5], diag[7]])
    between()
    g01 = dot(below[1], n0)
    g21 = t_dot(below[2], n2)
    g23 = dot(below[3], n2)
    g54 = t_dot(below[5], n5)
    g56 = dot(below[6], n5)
    g76 = t_dot(below[7], n7)
    d1 = diag[1] + dot_t(g01, below[1]) + dot(g21, below[2])
    d6 = diag[6] + dot_t(g56, below[6]) + dot(g76, below[7])
    d3 = diag[3] + dot_t(g23, below[3])
    d4 = diag[4] + dot(g54, below[5])
    f31 = dot(g23, below[2])
    f64 = dot(g56, below[5])
    n1, n6 = minus_inverse([d1, d6])
    g13 = dot(f31, n1)
    g64 = t_dot(f64, n6)
    d3 = d3 + dot_t(g13, f31)
    d4 = d4 + dot(g64, f64)
    (n3,) = minus_inverse([d3])
    g34 = dot(below[4], n3)
    d4 = d4 + dot_t(g34, below[4])
    panel_ready()
    for k in range(PBLK):
        for i in range(2):
            p_ref[k, :, i * BLK : i * BLK + BLK] = left_ref[i, k].astype(F32)
        for j in range(4):
            p_ref[k, :, (2 + j) * BLK : (3 + j) * BLK] = right_ref[k, j].astype(F32)
    couple(g01, 0, 1)
    couple(g21, 2, 1)
    couple(g23, 2, 3)
    couple(g54, 5, 4)
    couple(g56, 5, 6)
    couple(g76, 7, 6)
    couple(g13, 1, 3)
    couple(g64, 6, 4)
    couple(g34, 3, 4)
    (n4,) = minus_inverse([d4])
    total = None
    for k, minus in ((0, n0), (1, n1), (2, n2), (3, n3), (5, n5), (6, n6), (7, n7), (4, n4)):
        solved = dot(minus, p_ref[k, :, 2 * BLK :])
        part = t_dot(p_ref[k, :, : 2 * BLK], solved)
        total = part if total is None else total + part
    out_ref[...] = total


def device(x, h, l, z, c):
    return {"rec": x * 2 + h, "row": l, "col": z * 2 + c}


def remote(src, dst, send_sem, recv_sem, to):
    return pltpu.make_async_remote_copy(
        src_ref=src,
        dst_ref=dst,
        send_sem=send_sem,
        recv_sem=recv_sem,
        device_id=to,
        device_id_type=MESH,
    )


def loop(low, high, step):
    def one(at, carry):
        step(at)
        return carry

    lax.fori_loop(low, high, one, 0)


def main_kernel(
    first, count, loc, glo, wts, out,
    t_in, p_in, t_out, left, right, solve, tc, ts, tz1, ty1, tz2, ty2, tx, half2, half3, px, pa, pp, py, pc,
    s_tc, r_tc, s_z1, r_z1, s_y1, r_y1, s_z2, r_z2, s_y2, r_y2, s_tx, r_tx,
    s_z3, r_z3, s_y3, r_y3, s_f, r_f, s_px, r_px, s_py, r_py,
    s_rg, r_rg, s_lg, r_lg, s_ry, r_ry, s_rx, r_rx, s_lz, r_lz, s_lc, r_lc,
):
    rec, l, col = lax.axis_index("rec"), lax.axis_index("row"), lax.axis_index("col")
    x, h, z, c = rec // 2, rec % 2, col // 2, col % 2
    y = h * 4 + l
    me = device(x, h, l, z, c)
    pair = device(x, h, l, z, 1 - c)
    partner = device(x, 1 - h, l, z, c)

    def at_z(i):
        return device(x, h, l, i, c)

    def at_y(i):
        return device(x, i // 4, i % 4, z, c)

    def at_x(i):
        return device(i, h, l, z, c)

    mine = 2 * x + h
    right_source = z // 2 == l
    left_source = y == z
    right_z, right_c, right_j = 2 * l + z // 4, (z % 4) // 2, 2 * (z % 2) + c
    right_home = (right_z == z) & (right_c == c)
    right_to = device(x, h, l, right_z, right_c)
    left_home = (l == x) & (z == y)
    left_to = device(l, z // 4, z % 4, z, c)

    barrier = pltpu.get_barrier_semaphore()

    def greet(to):
        pl.semaphore_signal(barrier, inc=1, device_id=to, device_id_type=MESH)

    greet(pair)
    loop(1, 8, lambda d: greet(at_z((z + d) % 8)))
    loop(1, 8, lambda d: greet(at_y((y + d) % 8)))
    loop(1, 4, lambda d: greet(at_x((x + d) % 4)))

    @pl.when(right_source)
    def _():
        for j in range(4):
            from_z, from_c = 4 * (z % 2) + 2 * c + j // 2, j % 2

            @pl.when((from_z != z) | (from_c != c))
            def _():
                greet(device(x, h, l, from_z, from_c))

    @pl.when(left_source)
    def _():
        for k in range(8):

            @pl.when((k != mine) | (l != x))
            def _():
                greet(device(k // 2, k % 2, x, z, c))

    bundle_terms(first, count, loc, glo, wts, t_in, p_in)
    away = jnp.where(right_home, 0, 1) + jnp.where(left_home, 0, 1)
    pl.semaphore_wait(barrier, 18 + away)

    copy_tc = remote(t_in.at[1 - c], tc, s_tc, r_tc, pair)
    copy_tc.start()

    def panel_x(d):
        to = (x + d) % 4
        return remote(p_in.at[pl.ds(2 * to, 2)], px.at[d], s_px.at[d], r_px.at[d], at_x(to))

    loop(1, 4, lambda d: panel_x(d).start())

    copy_tc.wait_recv()

    def pair_sum(i):
        ts[i] = (t_in[c, i].astype(F32) + tc[i].astype(F32)).astype(BF16)

    loop(0, 8, pair_sum)

    def send_z1(d):
        to = (z + d) % 8
        return remote(ts.at[to, pl.ds(0, HALF)], tz1.at[d], s_z1.at[d], r_z1.at[d], at_z(to))

    def send_y1(d):
        to = (y + d) % 8
        return remote(ts.at[to, pl.ds(HALF, HALF)], ty1.at[d], s_y1.at[d], r_y1.at[d], at_y(to))

    def start_1(d):
        send_z1(d).start()
        send_y1(d).start()

    loop(1, 8, start_1)

    for d in range(1, 4):
        panel_x(d).wait_recv()
    for hh in range(2):
        total = p_in[2 * x + hh].astype(F32)
        for d in range(1, 4):
            total = total + px[d, hh].astype(F32)
        pa[hh] = total
    pp[...] = pa[1 - h].astype(BF16)
    copy_py = remote(pp, py, s_py, r_py, partner)
    copy_py.start()

    def wait_1(d):
        send_z1(d).wait_recv()
        send_y1(d).wait_recv()

    loop(1, 8, wait_1)
    sum_z = ts[z, 0:HALF].astype(F32)
    sum_y = ts[y, HALF:BLK].astype(F32)
    for d in range(1, 8):
        sum_z = sum_z + tz1[d].astype(F32)
        sum_y = sum_y + ty1[d].astype(F32)
    half2[0] = sum_z.astype(BF16)
    half2[1] = sum_y.astype(BF16)

    def send_y2(d):
        to = (y + d) % 8
        return remote(half2.at[0], ty2.at[d], s_y2.at[d], r_y2.at[d], at_y(to))

    def send_z2(d):
        to = (z + d) % 8
        return remote(half2.at[1], tz2.at[d], s_z2.at[d], r_z2.at[d], at_z(to))

    def start_2(d):
        send_y2(d).start()
        send_z2(d).start()

    loop(1, 8, start_2)

    copy_py.wait_recv()
    piece = (pa[h] + py[...].astype(F32)).astype(BF16)
    pc[...] = piece
    copy_rg = remote(pc, right.at[mine, right_j], s_rg, r_rg.at[right_j], right_to)
    copy_lg = remote(pc, left.at[c, mine], s_lg, r_lg.at[mine], left_to)

    @pl.when(right_home)
    def _():
        right[mine, right_j] = piece

    @pl.when(jnp.logical_not(right_home))
    def _():
        copy_rg.start()

    @pl.when(left_home)
    def _():
        left[c, mine] = piece

    @pl.when(jnp.logical_not(left_home))
    def _():
        copy_lg.start()

    def wait_2(d):
        send_y2(d).wait_recv()
        send_z2(d).wait_recv()

    loop(1, 8, wait_2)
    sum_z = half2[0].astype(F32)
    sum_y = half2[1].astype(F32)
    for d in range(1, 8):
        sum_z = sum_z + ty2[d].astype(F32)
        sum_y = sum_y + tz2[d].astype(F32)
    half3[0] = sum_z
    half3[1] = sum_y

    def send_tx(d):
        return remote(half3, tx.at[d], s_tx.at[d], r_tx.at[d], at_x((x + d) % 4))

    loop(1, 4, lambda d: send_tx(d).start())
    loop(1, 4, lambda d: send_tx(d).wait_recv())
    sum_z, sum_y = half3[0], half3[1]
    for d in range(1, 4):
        sum_z = sum_z + tx[d, 0]
        sum_y = sum_y + tx[d, 1]
    t_out[c, z, 0:HALF] = sum_z
    t_out[c, y, HALF:BLK] = sum_y

    def upper(cc, i):
        return t_out.at[cc, i, pl.ds(0, HALF)]

    def lower(cc, i):
        return t_out.at[cc, i, pl.ds(HALF, HALF)]

    def send_z3(d):
        return remote(upper(c, z), upper(c, z), s_z3.at[d], r_z3.at[d], at_z((z + d) % 8))

    def send_y3(d):
        return remote(lower(c, y), lower(c, y), s_y3.at[d], r_y3.at[d], at_y((y + d) % 8))

    def got_z3(d):
        i = (z + 8 - d) % 8
        return remote(upper(c, i), upper(c, i), s_z3.at[d], r_z3.at[d], at_z(i))

    def got_y3(d):
        i = (y + 8 - d) % 8
        return remote(lower(c, i), lower(c, i), s_y3.at[d], r_y3.at[d], at_y(i))

    def across_z(cc, i):
        return remote(upper(cc, i), upper(cc, i), s_f.at[i], r_f.at[i], pair)

    def across_y(cc, i):
        return remote(lower(cc, i), lower(cc, i), s_f.at[8 + i], r_f.at[8 + i], pair)

    def start_3(d):
        send_z3(d).start()
        send_y3(d).start()

    loop(1, 8, start_3)
    across_z(c, z).start()
    across_y(c, y).start()

    def right_y(d):
        return remote(right.at[mine], right.at[mine], s_ry.at[d], r_ry.at[h], at_y((y + d) % 8))

    def left_z(d):
        return remote(left.at[c], left.at[c], s_lz.at[d], r_lz, at_z((z + d) % 8))

    @pl.when(right_source)
    def _():
        for j in range(4):
            from_z, from_c = 4 * (z % 2) + 2 * c + j // 2, j % 2

            @pl.when((from_z != z) | (from_c != c))
            def _():
                remote(pc, right.at[mine, j], s_rg, r_rg.at[j], device(x, h, l, from_z, from_c)).wait_recv()

        loop(1, 8, lambda d: right_y(d).start())

    @pl.when(left_source)
    def _():
        for k in range(8):

            @pl.when((k != mine) | (l != x))
            def _():
                remote(pc, left.at[c, k], s_lg, r_lg.at[k], device(k // 2, k % 2, x, z, c)).wait_recv()

        loop(1, 8, lambda d: left_z(d).start())

    def arrived_3(d):
        got_z3(d).wait_recv()
        across_z(c, (z + 8 - d) % 8).start()
        got_y3(d).wait_recv()
        across_y(c, (y + 8 - d) % 8).start()

    loop(1, 8, arrived_3)

    def across(i):
        across_z(1 - c, i).wait_recv()
        across_y(1 - c, i).wait_recv()

    loop(0, 8, across)

    def right_x(hh, d):
        block = right.at[2 * x + hh]
        at = hh * 4 + d
        return remote(block, block, s_rx.at[at], r_rx.at[at], at_x((x + d) % 4))

    copy_lc = remote(left.at[c], left.at[c], s_lc, r_lc, pair)

    def pass_on():
        for hh in range(2):
            source = 4 * hh + z // 2

            @pl.when(y != source)
            def _():
                block = right.at[2 * x + hh]
                remote(block, block, s_ry.at[0], r_ry.at[hh], at_y(source)).wait_recv()

            loop(1, 4, lambda d: right_x(hh, d).start())

        @pl.when(y != z)
        def _():
            remote(left.at[c], left.at[c], s_lz.at[0], r_lz, at_z(y)).wait_recv()

        copy_lc.start()

    def panel_ready():
        remote(left.at[1 - c], left.at[1 - c], s_lc, r_lc, pair).wait_recv()
        for hh in range(2):

            def got_x(d):
                i = (x + 4 - d) % 4
                block = right.at[2 * i + hh]
                at = hh * 4 + d
                remote(block, block, s_rx.at[at], r_rx.at[at], at_x(i)).wait_recv()

            loop(1, 4, got_x)

    eliminate(t_out, left, right, out, solve, pass_on, panel_ready)

    copy_tc.wait_send()
    copy_py.wait_send()
    copy_lc.wait_send()

    @pl.when(jnp.logical_not(right_home))
    def _():
        copy_rg.wait_send()

    @pl.when(jnp.logical_not(left_home))
    def _():
        copy_lg.wait_send()

    def sent_7(d):
        send_z1(d).wait_send()
        send_y1(d).wait_send()
        send_z2(d).wait_send()
        send_y2(d).wait_send()
        send_z3(d).wait_send()
        send_y3(d).wait_send()

    loop(1, 8, sent_7)

    def sent_3(d):
        panel_x(d).wait_send()
        send_tx(d).wait_send()
        right_x(0, d).wait_send()
        right_x(1, d).wait_send()

    loop(1, 4, sent_3)

    def sent_8(i):
        across_z(c, i).wait_send()
        across_y(c, i).wait_send()

    loop(0, 8, sent_8)

    @pl.when(right_source)
    def _():
        loop(1, 8, lambda d: right_y(d).wait_send())

    @pl.when(left_source)
    def _():
        loop(1, 8, lambda d: left_z(d).wait_send())


def body(local_derivs, global_derivs, weights, first_block, bundle_count, trailing_block):
    vmem = pl.BlockSpec(memory_space=pltpu.VMEM)
    smem = pl.BlockSpec(memory_space=pltpu.SMEM)
    block = (BLK, BLK)
    shape = jax.ShapeDtypeStruct
    dma = pltpu.SemaphoreType.DMA
    half = (HALF, BLK)
    sems = (
        [dma, dma]
        + [dma((8,))] * 8
        + [dma((4,))] * 2
        + [dma((8,))] * 4
        + [dma((16,))] * 2
        + [dma((4,))] * 2
        + [dma, dma]
        + [dma, dma((4,)), dma, dma((8,))]
        + [dma((8,)), dma((2,)), dma((8,)), dma((8,))]
        + [dma((8,)), dma, dma, dma]
    )
    delta = pl.pallas_call(
        main_kernel,
        name="normal",
        in_specs=[smem, smem, vmem, vmem, vmem],
        out_specs=vmem,
        out_shape=shape(trailing_block.shape, F32),
        scratch_shapes=[
            pltpu.VMEM((2, PBLK) + block, BF16),
            pltpu.VMEM((PBLK,) + block, BF16),
            pltpu.VMEM((2, PBLK) + block, F32),
            pltpu.VMEM((2, PBLK) + block, BF16),
            pltpu.VMEM((PBLK, 4) + block, BF16),
            pltpu.VMEM((PBLK, BLK, 6 * BLK), F32),
            pltpu.VMEM((PBLK,) + block, BF16),
            pltpu.VMEM((PBLK,) + block, BF16),
            pltpu.VMEM((8,) + half, BF16),
            pltpu.VMEM((8,) + half, BF16),
            pltpu.VMEM((8,) + half, BF16),
            pltpu.VMEM((8,) + half, BF16),
            pltpu.VMEM((4, 2) + half, F32),
            pltpu.VMEM((2,) + half, BF16),
            pltpu.VMEM((2,) + half, F32),
            pltpu.VMEM((4, 2) + block, BF16),
            pltpu.VMEM((2,) + block, F32),
            pltpu.VMEM(block, BF16),
            pltpu.VMEM(block, BF16),
            pltpu.VMEM(block, BF16),
        ]
        + sems,
        compiler_params=pltpu.CompilerParams(collective_id=0, has_side_effects=True),
    )(first_block, bundle_count, local_derivs, global_derivs, weights)
    return trailing_block + delta


def solution(mesh):
    return jax.shard_map(
        body,
        mesh=mesh,
        in_specs=(
            P(("rec", "row", "col"), None, None),
            P(("rec", "row", "col"), None, None),
            P(("rec", "row", "col"), None),
            P(("rec", "row", "col")),
            P(("rec", "row", "col")),
            P(("rec", "row"), "col"),
        ),
        out_specs=P(("rec", "row"), "col"),
        check_vma=False,
    )
```

```python
import functools

import jax
import jax.numpy as jnp
from jax import lax
from jax.experimental import pallas as pl
from jax.experimental.pallas import tpu as pltpu
from jax.sharding import PartitionSpec as P

HIGH = lax.Precision.HIGHEST
MESH = pl.DeviceIdType.MESH
BLK = 128
PBLK = 8
HALF = BLK // 2
STRIPS = 4
F32 = jnp.float32
BF16 = jnp.bfloat16


def recip(x):
    r = pl.reciprocal(x, approx=True)
    return r * (2.0 - x * r)


def row(v, i):
    return jnp.broadcast_to(v[..., i:i + 1, :], v.shape)


def tree(v):
    while v.shape[0] > 1:
        half = v.shape[0] // 2
        v = v[:half] + v[half:]
    return v[0]


def strip_sweep(strips, j, base, sub, lan):
    inside = (lan >= base) & (lan < base + 8)
    panel = strips[j]
    shape = panel.shape

    def columns(s):
        return [jnp.broadcast_to(s[:, :, base + k:base + k + 1], shape) for k in range(8)]

    others = [o for o in range(len(strips)) if o != j]
    state = columns(panel)
    outer = [columns(strips[o]) for o in others]
    state = jnp.stack(state + [jnp.where(inside, jnp.where(lan - base == sub, -1.0, 0.0), panel)])
    for i in range(0, 8, 2):
        c0, c1 = state[0], state[1]
        a, b, c = row(c0, i), row(c0, i + 1), row(c1, i + 1)
        rd = recip(a * c - b * b)
        v = state[2:]
        p, q = row(v, i), row(v, i + 1)
        u = (c * rd) * p - (b * rd) * q
        w = (a * rd) * q - (b * rd) * p
        state = jnp.where(sub == i, u, jnp.where(sub == i + 1, w, v - (c0 * u + c1 * w)))
    x = state[0]
    rows = jnp.stack([row(x, k) for k in range(8)])
    new = list(strips)
    for at, o in enumerate(others):
        new[o] = jnp.where(inside, 0.0, strips[o]) - tree(jnp.stack(outer[at]) * rows)
    new[j] = x
    return new


def minus_inverse(mats):
    n = mats[0].shape[0]
    eye = lax.broadcasted_iota(jnp.int32, (n, n), 0) == lax.broadcasted_iota(jnp.int32, (n, n), 1)
    scales = []
    for a in mats:
        only = jnp.where(eye, a, 0.0)
        down = lax.rsqrt(jnp.sum(only, axis=1, keepdims=True))
        across = lax.rsqrt(jnp.sum(only, axis=0, keepdims=True))
        scales.append((down, across))
    mats = [a * down * across for a, (down, across) in zip(mats, scales)]
    h = 8 * STRIPS
    sub = lax.broadcasted_iota(jnp.int32, (8, n), 0)
    lan = lax.broadcasted_iota(jnp.int32, (8, n), 1)
    wide = lax.broadcasted_iota(jnp.int32, (n, n), 1)
    for low in range(0, n, h):
        strips = [jnp.stack([a[low + 8 * s:low + 8 * s + 8, :] for a in mats]) for s in range(STRIPS)]
        for s in range(STRIPS):
            strips = strip_sweep(strips, s, low + 8 * s, sub, lan)
        out = []
        for m, a in enumerate(mats):
            w = jnp.concatenate([s[m] for s in strips], axis=0)
            above = [jnp.zeros((low, n), F32)] if low else []
            below = [jnp.zeros((n - low - h, n), F32)] if low + h < n else []
            pad = jnp.concatenate(above + [w] + below, axis=0)
            keep = jnp.where((wide >= low) & (wide < low + h), 0.0, a)
            new = keep - jnp.dot(a, pad, precision=HIGH, preferred_element_type=F32)
            parts = ([new[:low]] if low else []) + [w] + ([new[low + h:]] if low + h < n else [])
            out.append(jnp.concatenate(parts, axis=0))
        mats = out
    return [a * down * across for a, (down, across) in zip(mats, scales)]


def contract(a, b, da, db):
    return lax.dot_general(a, b, (((da,), (db,)), ((), ())), preferred_element_type=F32)


def split(a):
    if a.dtype == BF16:
        return a, None
    high = a.astype(BF16)
    return high, (a - high.astype(F32)).astype(BF16)


def product(a, b, da=1, db=0):
    (ah, al), (bh, bl) = a, b
    total = contract(ah, bh, da, db)
    if bl is not None:
        total = total + contract(ah, bl, da, db)
    if al is not None:
        total = total + contract(al, bh, da, db)
    return total


def bundle_grams(loc_ref, glo_ref, wts_ref):
    grams = []
    for b in range(loc_ref.shape[0]):
        columns = []
        for part in range(loc_ref.shape[1] // BLK):
            w = jnp.sqrt(wts_ref[b : b + 1, part * BLK : part * BLK + BLK])
            columns.append(jnp.transpose(jnp.broadcast_to(w, (8, BLK)))[:, 0:1])
        root = jnp.concatenate(columns, axis=0)
        sl = (root * loc_ref[b].astype(F32)).astype(BF16)
        sg = (root * glo_ref[b].astype(F32)).astype(BF16)
        pair = sg[:, : 2 * BLK]
        grams.append(
            (
                contract(sl, sl, 0, 0),
                split(contract(sl, sg, 0, 0)),
                contract(pair, pair, 0, 0),
                contract(sg[:, 2 * BLK :], pair, 0, 0),
            )
        )
    return grams


def flags(first_ref, count_ref, b, k):
    live = (b < count_ref[0]).astype(F32)
    first = (first_ref[b] == k).astype(F32) * live
    second = (first_ref[b] + 1 == k).astype(F32) * live
    return first, second


def bundle_blocks(first_ref, count_ref, grams, fitted, t_ref):
    reduced = []
    for (_, cross, pair, _), fit in zip(grams, fitted):
        two = tuple(v[:, : 2 * BLK] for v in cross)
        reduced.append(pair + product(two, fit, 0, 0))
    for k in range(PBLK):
        diag = jnp.zeros((BLK, BLK), F32)
        below = jnp.zeros((BLK, BLK), F32)
        for b, r in enumerate(reduced):
            first, second = flags(first_ref, count_ref, b, k)
            if k < PBLK - 1:
                diag = diag + first * r[:BLK, :BLK]
            if k > 0:
                diag = diag + second * r[BLK:, BLK:]
                below = below + second * r[BLK:, :BLK]
        t_ref[0, k] = diag.astype(BF16)
        t_ref[1, k] = below.astype(BF16)


def bundle_panel(first_ref, count_ref, grams, fitted, p_ref):
    reduced = []
    for (_, cross, _, side), fit in zip(grams, fitted):
        third = tuple(v[:, 2 * BLK :] for v in cross)
        reduced.append(side + product(third, fit, 0, 0))
    for k in range(PBLK):
        rhs = jnp.zeros((BLK, BLK), F32)
        for b, r in enumerate(reduced):
            first, second = flags(first_ref, count_ref, b, k)
            if k < PBLK - 1:
                rhs = rhs + first * r[:, :BLK]
            if k > 0:
                rhs = rhs + second * r[:, BLK:]
        p_ref[k] = rhs.astype(BF16)


def eliminate(t_ref, left_ref, right_ref, out_ref, between, panel_ready):
    diag = [t_ref[0, k] for k in range(PBLK)]
    below = [None] + [split(t_ref[1, k]) for k in range(1, PBLK)]

    n0, n2, n5, n7 = [split(n) for n in minus_inverse([diag[0], diag[2], diag[5], diag[7]])]
    between()
    g01 = split(product(below[1], n0))
    g21 = split(product(below[2], n2, 0, 0))
    g23 = split(product(below[3], n2))
    g54 = split(product(below[5], n5, 0, 0))
    g56 = split(product(below[6], n5))
    g76 = split(product(below[7], n7, 0, 0))
    d1 = diag[1] + product(g01, below[1], 1, 1) + product(g21, below[2])
    d6 = diag[6] + product(g56, below[6], 1, 1) + product(g76, below[7])
    d3 = diag[3] + product(g23, below[3], 1, 1)
    d4 = diag[4] + product(g54, below[5])
    f31 = split(product(g23, below[2]))
    f64 = split(product(g56, below[5]))
    n1, n6 = [split(n) for n in minus_inverse([d1, d6])]
    g13 = split(product(f31, n1))
    g64 = split(product(f64, n6, 0, 0))
    d3 = d3 + product(g13, f31, 1, 1)
    d4 = d4 + product(g64, f64)
    n3 = split(minus_inverse([d3])[0])
    g34 = split(product(below[4], n3))
    d4 = d4 + product(g34, below[4], 1, 1)
    panel_ready()

    def panel(k):
        parts = [left_ref[i, k] for i in range(2)] + [right_ref[k, j] for j in range(4)]
        return jnp.concatenate(parts, axis=0)

    def onto(k, *pairs):
        total = panel(k).astype(F32)
        for source, gain in pairs:
            total = total + product(source, gain, 1, 1)
        return split(total)

    p0, p2, p5, p7 = [split(panel(k)) for k in (0, 2, 5, 7)]
    p1 = onto(1, (p0, g01), (p2, g21))
    p6 = onto(6, (p5, g56), (p7, g76))
    p3 = onto(3, (p2, g23), (p1, g13))
    p4 = onto(4, (p5, g54), (p6, g64), (p3, g34))

    def sides(p):
        cut = 2 * BLK
        return [tuple(None if v is None else v[at] for v in p) for at in (slice(0, cut), slice(cut, None))]

    def update(blocks):
        lefts, rights = [], []
        for p, n in blocks:
            one, other = sides(p)
            low = jnp.zeros_like(one[0]) if one[1] is None else one[1]
            lefts.append((one[0], low))
            rights.append(split(product(other, n)))
        high_l, low_l = [jnp.concatenate(v, axis=1) for v in zip(*lefts)]
        high_r, low_r = [jnp.concatenate(v, axis=1) for v in zip(*rights)]
        return product((high_l, low_l), (high_r, low_r), 1, 1)

    early = update([(p0, n0), (p1, n1), (p2, n2), (p3, n3), (p5, n5), (p6, n6)])
    n4 = split(minus_inverse([d4])[0])
    out_ref[...] = early + update([(p4, n4), (p7, n7)])


def device(x, h, l, z, c):
    return {"rec": x * 2 + h, "row": l, "col": z * 2 + c}


def remote(src, dst, send_sem, recv_sem, to):
    return pltpu.make_async_remote_copy(
        src_ref=src,
        dst_ref=dst,
        send_sem=send_sem,
        recv_sem=recv_sem,
        device_id=to,
        device_id_type=MESH,
    )


def loop(low, high, step):
    def one(at, carry):
        step(at)
        return carry

    lax.fori_loop(low, high, one, 0)


def main_kernel(
    first, count, loc, glo, wts, out,
    t_in, p_in, t_out, left, right, tc, ts, tz1, ty1, tz2, ty2, tx, half2, half3, px, pa, pp, py, pc,
    s_tc, r_tc, s_z1, r_z1, s_y1, r_y1, s_z2, r_z2, s_y2, r_y2, s_tx, r_tx,
    s_z3, r_z3, s_y3, r_y3, s_f, r_f, s_px, r_px, s_py, r_py,
    s_rg, r_rg, s_lg, r_lg, s_ry, r_ry, s_rx, r_rx, s_lz, r_lz, s_lc, r_lc,
):
    rec, l, col = lax.axis_index("rec"), lax.axis_index("row"), lax.axis_index("col")
    x, h, z, c = rec // 2, rec % 2, col // 2, col % 2
    y = h * 4 + l
    me = device(x, h, l, z, c)
    pair = device(x, h, l, z, 1 - c)
    partner = device(x, 1 - h, l, z, c)

    def at_z(i):
        return device(x, h, l, i, c)

    def at_y(i):
        return device(x, i // 4, i % 4, z, c)

    def at_x(i):
        return device(i, h, l, z, c)

    mine = 2 * x + h
    right_source = z // 2 == l
    left_source = y == z
    right_z, right_c, right_j = 2 * l + z // 4, (z % 4) // 2, 2 * (z % 2) + c
    right_home = (right_z == z) & (right_c == c)
    right_to = device(x, h, l, right_z, right_c)
    left_home = (l == x) & (z == y)
    left_to = device(l, z // 4, z % 4, z, c)

    barrier = pltpu.get_barrier_semaphore()

    def greet(to):
        pl.semaphore_signal(barrier, inc=1, device_id=to, device_id_type=MESH)

    greet(pair)
    loop(1, 8, lambda d: greet(at_z((z + d) % 8)))
    loop(1, 8, lambda d: greet(at_y((y + d) % 8)))
    loop(1, 4, lambda d: greet(at_x((x + d) % 4)))

    @pl.when(right_source)
    def _():
        for j in range(4):
            from_z, from_c = 4 * (z % 2) + 2 * c + j // 2, j % 2

            @pl.when((from_z != z) | (from_c != c))
            def _():
                greet(device(x, h, l, from_z, from_c))

    @pl.when(left_source)
    def _():
        for k in range(8):

            @pl.when((k != mine) | (l != x))
            def _():
                greet(device(k // 2, k % 2, x, z, c))

    grams = bundle_grams(loc, glo, wts)
    minus = [split(n) for n in minus_inverse([g[0] for g in grams])]
    fitted = [
        split(product(n, tuple(v[:, : 2 * BLK] for v in g[1]))) for n, g in zip(minus, grams)
    ]
    bundle_blocks(first, count, grams, fitted, t_in)
    away = jnp.where(right_home, 0, 1) + jnp.where(left_home, 0, 1)
    pl.semaphore_wait(barrier, 18 + away)

    def across_tc(i):
        return remote(t_in.at[1 - c, i], tc.at[i], s_tc.at[i], r_tc.at[i], pair)

    loop(0, 8, lambda i: across_tc(i).start())

    bundle_panel(first, count, grams, fitted, p_in)

    def panel_x(d):
        to = (x + d) % 4
        return remote(p_in.at[pl.ds(2 * to, 2)], px.at[d], s_px.at[d], r_px.at[d], at_x(to))

    loop(1, 4, lambda d: panel_x(d).start())

    def send_z1(d):
        to = (z + d) % 8
        return remote(ts.at[to, pl.ds(0, HALF)], tz1.at[d], s_z1.at[d], r_z1.at[d], at_z(to))

    def send_y1(d):
        to = (y + d) % 8
        return remote(ts.at[to, pl.ds(HALF, HALF)], ty1.at[d], s_y1.at[d], r_y1.at[d], at_y(to))

    def start_1(i):
        across_tc(i).wait_recv()
        ts[i] = (t_in[c, i].astype(F32) + tc[i].astype(F32)).astype(BF16)

        @pl.when(i != z)
        def _():
            send_z1((i + 8 - z) % 8).start()

        @pl.when(i != y)
        def _():
            send_y1((i + 8 - y) % 8).start()

    loop(0, 8, start_1)

    for d in range(1, 4):
        panel_x(d).wait_recv()
    for hh in range(2):
        total = p_in[2 * x + hh].astype(F32)
        for d in range(1, 4):
            total = total + px[d, hh].astype(F32)
        pa[hh] = total
    pp[...] = pa[1 - h].astype(BF16)
    copy_py = remote(pp, py, s_py, r_py, partner)
    copy_py.start()

    def wait_1(d):
        send_z1(d).wait_recv()
        send_y1(d).wait_recv()

    loop(1, 8, wait_1)
    sum_z = ts[z, 0:HALF].astype(F32)
    sum_y = ts[y, HALF:BLK].astype(F32)
    for d in range(1, 8):
        sum_z = sum_z + tz1[d].astype(F32)
        sum_y = sum_y + ty1[d].astype(F32)
    half2[0] = sum_z.astype(BF16)
    half2[1] = sum_y.astype(BF16)

    def send_y2(d):
        to = (y + d) % 8
        return remote(half2.at[0], ty2.at[d], s_y2.at[d], r_y2.at[d], at_y(to))

    def send_z2(d):
        to = (z + d) % 8
        return remote(half2.at[1], tz2.at[d], s_z2.at[d], r_z2.at[d], at_z(to))

    def start_2(d):
        send_y2(d).start()
        send_z2(d).start()

    loop(1, 8, start_2)

    copy_py.wait_recv()
    piece = (pa[h] + py[...].astype(F32)).astype(BF16)
    pc[...] = piece
    copy_rg = remote(pc, right.at[mine, right_j], s_rg, r_rg.at[right_j], right_to)
    copy_lg = remote(pc, left.at[c, mine], s_lg, r_lg.at[mine], left_to)

    @pl.when(right_home)
    def _():
        right[mine, right_j] = piece

    @pl.when(jnp.logical_not(right_home))
    def _():
        copy_rg.start()

    @pl.when(left_home)
    def _():
        left[c, mine] = piece

    @pl.when(jnp.logical_not(left_home))
    def _():
        copy_lg.start()

    def wait_2(d):
        send_y2(d).wait_recv()
        send_z2(d).wait_recv()

    loop(1, 8, wait_2)
    sum_z = half2[0].astype(F32)
    sum_y = half2[1].astype(F32)
    for d in range(1, 8):
        sum_z = sum_z + ty2[d].astype(F32)
        sum_y = sum_y + tz2[d].astype(F32)
    half3[0] = sum_z.astype(BF16)
    half3[1] = sum_y.astype(BF16)

    def send_tx(d):
        return remote(half3, tx.at[d], s_tx.at[d], r_tx.at[d], at_x((x + d) % 4))

    loop(1, 4, lambda d: send_tx(d).start())
    loop(1, 4, lambda d: send_tx(d).wait_recv())
    sum_z, sum_y = half3[0].astype(F32), half3[1].astype(F32)
    for d in range(1, 4):
        sum_z = sum_z + tx[d, 0].astype(F32)
        sum_y = sum_y + tx[d, 1].astype(F32)
    t_out[c, z, 0:HALF] = sum_z
    t_out[c, y, HALF:BLK] = sum_y

    def upper(cc, i):
        return t_out.at[cc, i, pl.ds(0, HALF)]

    def lower(cc, i):
        return t_out.at[cc, i, pl.ds(HALF, HALF)]

    def send_z3(d):
        return remote(upper(c, z), upper(c, z), s_z3.at[d], r_z3.at[d], at_z((z + d) % 8))

    def send_y3(d):
        return remote(lower(c, y), lower(c, y), s_y3.at[d], r_y3.at[d], at_y((y + d) % 8))

    def got_z3(d):
        i = (z + 8 - d) % 8
        return remote(upper(c, i), upper(c, i), s_z3.at[d], r_z3.at[d], at_z(i))

    def got_y3(d):
        i = (y + 8 - d) % 8
        return remote(lower(c, i), lower(c, i), s_y3.at[d], r_y3.at[d], at_y(i))

    def across_z(cc, i):
        return remote(upper(cc, i), upper(cc, i), s_f.at[i], r_f.at[i], pair)

    def across_y(cc, i):
        return remote(lower(cc, i), lower(cc, i), s_f.at[8 + i], r_f.at[8 + i], pair)

    def start_3(d):
        send_z3(d).start()
        send_y3(d).start()

    loop(1, 8, start_3)
    across_z(c, z).start()
    across_y(c, y).start()

    def right_y(d):
        return remote(right.at[mine], right.at[mine], s_ry.at[d], r_ry.at[h], at_y((y + d) % 8))

    def left_z(d):
        return remote(left.at[c], left.at[c], s_lz.at[d], r_lz, at_z((z + d) % 8))

    @pl.when(right_source)
    def _():
        for j in range(4):
            from_z, from_c = 4 * (z % 2) + 2 * c + j // 2, j % 2

            @pl.when((from_z != z) | (from_c != c))
            def _():
                remote(pc, right.at[mine, j], s_rg, r_rg.at[j], device(x, h, l, from_z, from_c)).wait_recv()

        loop(1, 8, lambda d: right_y(d).start())

    @pl.when(left_source)
    def _():
        for k in range(8):

            @pl.when((k != mine) | (l != x))
            def _():
                remote(pc, left.at[c, k], s_lg, r_lg.at[k], device(k // 2, k % 2, x, z, c)).wait_recv()

        loop(1, 8, lambda d: left_z(d).start())

    def arrived_3(d):
        got_z3(d).wait_recv()
        across_z(c, (z + 8 - d) % 8).start()
        got_y3(d).wait_recv()
        across_y(c, (y + 8 - d) % 8).start()

    loop(1, 8, arrived_3)

    def across(i):
        across_z(1 - c, i).wait_recv()
        across_y(1 - c, i).wait_recv()

    loop(0, 8, across)

    def right_x(hh, d):
        block = right.at[2 * x + hh]
        at = hh * 4 + d
        return remote(block, block, s_rx.at[at], r_rx.at[at], at_x((x + d) % 4))

    copy_lc = remote(left.at[c], left.at[c], s_lc, r_lc, pair)

    def pass_on():
        for hh in range(2):
            source = 4 * hh + z // 2

            @pl.when(y != source)
            def _():
                block = right.at[2 * x + hh]
                remote(block, block, s_ry.at[0], r_ry.at[hh], at_y(source)).wait_recv()

            loop(1, 4, lambda d: right_x(hh, d).start())

        @pl.when(y != z)
        def _():
            remote(left.at[c], left.at[c], s_lz.at[0], r_lz, at_z(y)).wait_recv()

        copy_lc.start()

    def panel_ready():
        remote(left.at[1 - c], left.at[1 - c], s_lc, r_lc, pair).wait_recv()
        for hh in range(2):

            def got_x(d):
                i = (x + 4 - d) % 4
                block = right.at[2 * i + hh]
                at = hh * 4 + d
                remote(block, block, s_rx.at[at], r_rx.at[at], at_x(i)).wait_recv()

            loop(1, 4, got_x)

    eliminate(t_out, left, right, out, pass_on, panel_ready)

    loop(0, 8, lambda i: across_tc(i).wait_send())
    copy_py.wait_send()
    copy_lc.wait_send()

    @pl.when(jnp.logical_not(right_home))
    def _():
        copy_rg.wait_send()

    @pl.when(jnp.logical_not(left_home))
    def _():
        copy_lg.wait_send()

    def sent_7(d):
        send_z1(d).wait_send()
        send_y1(d).wait_send()
        send_z2(d).wait_send()
        send_y2(d).wait_send()
        send_z3(d).wait_send()
        send_y3(d).wait_send()

    loop(1, 8, sent_7)

    def sent_3(d):
        panel_x(d).wait_send()
        send_tx(d).wait_send()
        right_x(0, d).wait_send()
        right_x(1, d).wait_send()

    loop(1, 4, sent_3)

    def sent_8(i):
        across_z(c, i).wait_send()
        across_y(c, i).wait_send()

    loop(0, 8, sent_8)

    @pl.when(right_source)
    def _():
        loop(1, 8, lambda d: right_y(d).wait_send())

    @pl.when(left_source)
    def _():
        loop(1, 8, lambda d: left_z(d).wait_send())


def body(local_derivs, global_derivs, weights, first_block, bundle_count, trailing_block):
    vmem = pl.BlockSpec(memory_space=pltpu.VMEM)
    smem = pl.BlockSpec(memory_space=pltpu.SMEM)
    block = (BLK, BLK)
    shape = jax.ShapeDtypeStruct
    dma = pltpu.SemaphoreType.DMA
    half = (HALF, BLK)
    sems = (
        [dma((8,))] * 10
        + [dma((4,))] * 2
        + [dma((8,))] * 4
        + [dma((16,))] * 2
        + [dma((4,))] * 2
        + [dma, dma]
        + [dma, dma((4,)), dma, dma((8,))]
        + [dma((8,)), dma((2,)), dma((8,)), dma((8,))]
        + [dma((8,)), dma, dma, dma]
    )
    delta = pl.pallas_call(
        main_kernel,
        name="normal",
        in_specs=[smem, smem, vmem, vmem, vmem],
        out_specs=vmem,
        out_shape=shape(trailing_block.shape, F32),
        scratch_shapes=[
            pltpu.VMEM((2, PBLK) + block, BF16),
            pltpu.VMEM((PBLK,) + block, BF16),
            pltpu.VMEM((2, PBLK) + block, F32),
            pltpu.VMEM((2, PBLK) + block, BF16),
            pltpu.VMEM((PBLK, 4) + block, BF16),
            pltpu.VMEM((PBLK,) + block, BF16),
            pltpu.VMEM((PBLK,) + block, BF16),
            pltpu.VMEM((8,) + half, BF16),
            pltpu.VMEM((8,) + half, BF16),
            pltpu.VMEM((8,) + half, BF16),
            pltpu.VMEM((8,) + half, BF16),
            pltpu.VMEM((4, 2) + half, BF16),
            pltpu.VMEM((2,) + half, BF16),
            pltpu.VMEM((2,) + half, BF16),
            pltpu.VMEM((4, 2) + block, BF16),
            pltpu.VMEM((2,) + block, F32),
            pltpu.VMEM(block, BF16),
            pltpu.VMEM(block, BF16),
            pltpu.VMEM(block, BF16),
        ]
        + sems,
        compiler_params=pltpu.CompilerParams(collective_id=0, has_side_effects=True),
    )(first_block, bundle_count, local_derivs, global_derivs, weights)
    return trailing_block + delta


def solution(mesh):
    return jax.shard_map(
        body,
        mesh=mesh,
        in_specs=(
            P(("rec", "row", "col"), None, None),
            P(("rec", "row", "col"), None, None),
            P(("rec", "row", "col"), None),
            P(("rec", "row", "col")),
            P(("rec", "row", "col")),
            P(("rec", "row"), "col"),
        ),
        out_specs=P(("rec", "row"), "col"),
        check_vma=False,
    )
```

```python
import functools

import jax
import jax.numpy as jnp
from jax import lax
from jax.experimental import pallas as pl
from jax.experimental.pallas import tpu as pltpu
from jax.sharding import PartitionSpec as P

HIGH = lax.Precision.HIGHEST
MESH = pl.DeviceIdType.MESH
BLK = 128
PBLK = 8
HALF = BLK // 2
STRIPS = 4
F32 = jnp.float32
BF16 = jnp.bfloat16


def recip(x):
    r = pl.reciprocal(x, approx=True)
    return r * (2.0 - x * r)


def row(v, i):
    return jnp.broadcast_to(v[..., i:i + 1, :], v.shape)


def tree(v):
    while v.shape[0] > 1:
        half = v.shape[0] // 2
        v = v[:half] + v[half:]
    return v[0]


def strip_sweep(strips, j, base, sub, lan):
    inside = (lan >= base) & (lan < base + 8)
    panel = strips[j]
    shape = panel.shape

    def columns(s):
        return [jnp.broadcast_to(s[:, :, base + k:base + k + 1], shape) for k in range(8)]

    others = [o for o in range(len(strips)) if o != j]
    state = columns(panel)
    outer = [columns(strips[o]) for o in others]
    state = jnp.stack(state + [jnp.where(inside, jnp.where(lan - base == sub, -1.0, 0.0), panel)])
    for i in range(0, 8, 2):
        c0, c1 = state[0], state[1]
        a, b, c = row(c0, i), row(c0, i + 1), row(c1, i + 1)
        rd = recip(a * c - b * b)
        v = state[2:]
        p, q = row(v, i), row(v, i + 1)
        u = (c * rd) * p - (b * rd) * q
        w = (a * rd) * q - (b * rd) * p
        state = jnp.where(sub == i, u, jnp.where(sub == i + 1, w, v - (c0 * u + c1 * w)))
    x = state[0]
    rows = jnp.stack([row(x, k) for k in range(8)])
    new = list(strips)
    for at, o in enumerate(others):
        new[o] = jnp.where(inside, 0.0, strips[o]) - tree(jnp.stack(outer[at]) * rows)
    new[j] = x
    return new


def minus_inverse(mats):
    n = mats[0].shape[0]
    eye = lax.broadcasted_iota(jnp.int32, (n, n), 0) == lax.broadcasted_iota(jnp.int32, (n, n), 1)
    scales = []
    for a in mats:
        only = jnp.where(eye, a, 0.0)
        down = lax.rsqrt(jnp.sum(only, axis=1, keepdims=True))
        across = lax.rsqrt(jnp.sum(only, axis=0, keepdims=True))
        scales.append((down, across))
    mats = [a * down * across for a, (down, across) in zip(mats, scales)]
    h = 8 * STRIPS
    sub = lax.broadcasted_iota(jnp.int32, (8, n), 0)
    lan = lax.broadcasted_iota(jnp.int32, (8, n), 1)
    wide = lax.broadcasted_iota(jnp.int32, (n, n), 1)
    for low in range(0, n, h):
        strips = [jnp.stack([a[low + 8 * s:low + 8 * s + 8, :] for a in mats]) for s in range(STRIPS)]
        for s in range(STRIPS):
            strips = strip_sweep(strips, s, low + 8 * s, sub, lan)
        out = []
        for m, a in enumerate(mats):
            w = jnp.concatenate([s[m] for s in strips], axis=0)
            above = [jnp.zeros((low, n), F32)] if low else []
            below = [jnp.zeros((n - low - h, n), F32)] if low + h < n else []
            pad = jnp.concatenate(above + [w] + below, axis=0)
            keep = jnp.where((wide >= low) & (wide < low + h), 0.0, a)
            new = keep - jnp.dot(a, pad, precision=HIGH, preferred_element_type=F32)
            parts = ([new[:low]] if low else []) + [w] + ([new[low + h:]] if low + h < n else [])
            out.append(jnp.concatenate(parts, axis=0))
        mats = out
    return [a * down * across for a, (down, across) in zip(mats, scales)]


def contract(a, b, da, db):
    return lax.dot_general(a, b, (((da,), (db,)), ((), ())), preferred_element_type=F32)


def split(a):
    if a.dtype == BF16:
        return a, None
    high = a.astype(BF16)
    return high, (a - high.astype(F32)).astype(BF16)


def product(a, b, da=1, db=0):
    (ah, al), (bh, bl) = a, b
    total = contract(ah, bh, da, db)
    if bl is not None:
        total = total + contract(ah, bl, da, db)
    if al is not None:
        total = total + contract(al, bh, da, db)
    return total


def bundle_grams(loc_ref, glo_ref, wts_ref):
    grams = []
    for b in range(loc_ref.shape[0]):
        columns = []
        for part in range(loc_ref.shape[1] // BLK):
            w = jnp.sqrt(wts_ref[b : b + 1, part * BLK : part * BLK + BLK])
            columns.append(jnp.transpose(jnp.broadcast_to(w, (8, BLK)))[:, 0:1])
        root = jnp.concatenate(columns, axis=0)
        sl = (root * loc_ref[b].astype(F32)).astype(BF16)
        sg = (root * glo_ref[b].astype(F32)).astype(BF16)
        pair = sg[:, : 2 * BLK]
        grams.append(
            (
                contract(sl, sl, 0, 0),
                split(contract(sl, sg, 0, 0)),
                contract(pair, pair, 0, 0),
                contract(sg[:, 2 * BLK :], pair, 0, 0),
            )
        )
    return grams


def flags(first_ref, count_ref, b, k):
    live = (b < count_ref[0]).astype(F32)
    first = (first_ref[b] == k).astype(F32) * live
    second = (first_ref[b] + 1 == k).astype(F32) * live
    return first, second


def bundle_blocks(first_ref, count_ref, grams, fitted, t_ref):
    reduced = []
    for (_, cross, pair, _), fit in zip(grams, fitted):
        two = tuple(v[:, : 2 * BLK] for v in cross)
        reduced.append(pair + product(two, fit, 0, 0))
    for k in range(PBLK):
        diag = jnp.zeros((BLK, BLK), F32)
        below = jnp.zeros((BLK, BLK), F32)
        for b, r in enumerate(reduced):
            first, second = flags(first_ref, count_ref, b, k)
            if k < PBLK - 1:
                diag = diag + first * r[:BLK, :BLK]
            if k > 0:
                diag = diag + second * r[BLK:, BLK:]
                below = below + second * r[BLK:, :BLK]
        t_ref[0, k] = diag.astype(BF16)
        t_ref[1, k] = below.astype(BF16)


def bundle_panel(first_ref, count_ref, grams, fitted, p_ref):
    reduced = []
    for (_, cross, _, side), fit in zip(grams, fitted):
        third = tuple(v[:, 2 * BLK :] for v in cross)
        reduced.append(side + product(third, fit, 0, 0))
    for k in range(PBLK):
        rhs = jnp.zeros((BLK, BLK), F32)
        for b, r in enumerate(reduced):
            first, second = flags(first_ref, count_ref, b, k)
            if k < PBLK - 1:
                rhs = rhs + first * r[:, :BLK]
            if k > 0:
                rhs = rhs + second * r[:, BLK:]
        p_ref[k] = rhs.astype(BF16)


def eliminate(t_ref, left_ref, right_ref, out_ref, between, panel_ready):
    diag = [t_ref[0, k] for k in range(PBLK)]
    below = [None] + [split(t_ref[1, k]) for k in range(1, PBLK)]

    n0, n2, n5, n7 = [split(n) for n in minus_inverse([diag[0], diag[2], diag[5], diag[7]])]
    between()
    g01 = split(product(below[1], n0))
    g21 = split(product(below[2], n2, 0, 0))
    g23 = split(product(below[3], n2))
    g54 = split(product(below[5], n5, 0, 0))
    g56 = split(product(below[6], n5))
    g76 = split(product(below[7], n7, 0, 0))
    d1 = diag[1] + product(g01, below[1], 1, 1) + product(g21, below[2])
    d6 = diag[6] + product(g56, below[6], 1, 1) + product(g76, below[7])
    d3 = diag[3] + product(g23, below[3], 1, 1)
    d4 = diag[4] + product(g54, below[5])
    f31 = split(product(g23, below[2]))
    f64 = split(product(g56, below[5]))
    n1, n6 = [split(n) for n in minus_inverse([d1, d6])]
    g13 = split(product(f31, n1))
    g64 = split(product(f64, n6, 0, 0))
    d3 = d3 + product(g13, f31, 1, 1)
    d4 = d4 + product(g64, f64)
    n3 = split(minus_inverse([d3])[0])
    g34 = split(product(below[4], n3))
    d4 = d4 + product(g34, below[4], 1, 1)
    panel_ready()

    def panel(k):
        parts = [left_ref[i, k] for i in range(2)] + [right_ref[k, j] for j in range(4)]
        return jnp.concatenate(parts, axis=0)

    def onto(k, *pairs):
        total = panel(k).astype(F32)
        for source, gain in pairs:
            total = total + product(source, gain, 1, 1)
        return split(total)

    p0, p2, p5, p7 = [split(panel(k)) for k in (0, 2, 5, 7)]
    p1 = onto(1, (p0, g01), (p2, g21))
    p6 = onto(6, (p5, g56), (p7, g76))
    p3 = onto(3, (p2, g23), (p1, g13))
    p4 = onto(4, (p5, g54), (p6, g64), (p3, g34))

    def sides(p):
        cut = 2 * BLK
        return [tuple(None if v is None else v[at] for v in p) for at in (slice(0, cut), slice(cut, None))]

    def update(blocks):
        lefts, rights = [], []
        for p, n in blocks:
            one, other = sides(p)
            low = jnp.zeros_like(one[0]) if one[1] is None else one[1]
            lefts.append((one[0], low))
            rights.append(split(product(other, n)))
        high_l, low_l = [jnp.concatenate(v, axis=1) for v in zip(*lefts)]
        high_r, low_r = [jnp.concatenate(v, axis=1) for v in zip(*rights)]
        return product((high_l, low_l), (high_r, low_r), 1, 1)

    early = update([(p0, n0), (p1, n1), (p2, n2), (p3, n3), (p5, n5), (p6, n6)])
    n4 = split(minus_inverse([d4])[0])
    out_ref[...] = early + update([(p4, n4), (p7, n7)])


def device(x, h, l, z, c):
    return {"rec": x * 2 + h, "row": l, "col": z * 2 + c}


def remote(src, dst, send_sem, recv_sem, to):
    return pltpu.make_async_remote_copy(
        src_ref=src,
        dst_ref=dst,
        send_sem=send_sem,
        recv_sem=recv_sem,
        device_id=to,
        device_id_type=MESH,
    )


def loop(low, high, step):
    def one(at, carry):
        step(at)
        return carry

    lax.fori_loop(low, high, one, 0)


def main_kernel(
    first, count, loc, glo, wts, out,
    t_in, p_in, t_out, left, right, tc, ts, tz1, ty1, tz2, ty2, tx, half2, half3, px, pa, pp, py, pc,
    s_tc, r_tc, s_z1, r_z1, s_y1, r_y1, s_z2, r_z2, s_y2, r_y2, s_tx, r_tx,
    s_z3, r_z3, s_y3, r_y3, s_f, r_f, s_px, r_px, s_py, r_py,
    s_rg, r_rg, s_lg, r_lg, s_ry, r_ry, s_rx, r_rx, s_lz, r_lz, s_lc, r_lc,
):
    rec, l, col = lax.axis_index("rec"), lax.axis_index("row"), lax.axis_index("col")
    x, h, z, c = rec // 2, rec % 2, col // 2, col % 2
    y = h * 4 + l
    me = device(x, h, l, z, c)
    pair = device(x, h, l, z, 1 - c)
    partner = device(x, 1 - h, l, z, c)

    def at_z(i):
        return device(x, h, l, i, c)

    def at_y(i):
        return device(x, i // 4, i % 4, z, c)

    def at_x(i):
        return device(i, h, l, z, c)

    mine = 2 * x + h
    right_z, right_c, right_j = 2 * l + z // 4, (z % 4) // 2, 2 * (z % 2) + c
    right_home = (right_j == l) & (right_z == z) & (right_c == c)
    right_to = device(x, h, right_j, right_z, right_c)
    right_from = device(x, h, z // 2, 4 * (z % 2) + 2 * c + l // 2, l % 2)
    left_home = (l == x) & (z == y) & (mine == z)
    left_to = device(l, z // 4, z % 4, mine, c)
    left_from = device(z // 2, z % 2, x, y, c)

    barrier = pltpu.get_barrier_semaphore()

    def greet(to):
        pl.semaphore_signal(barrier, inc=1, device_id=to, device_id_type=MESH)

    greet(pair)
    loop(1, 8, lambda d: greet(at_z((z + d) % 8)))
    loop(1, 8, lambda d: greet(at_y((y + d) % 8)))
    loop(1, 4, lambda d: greet(at_x((x + d) % 4)))

    @pl.when(jnp.logical_not(right_home))
    def _():
        greet(right_from)

    @pl.when(jnp.logical_not(left_home))
    def _():
        greet(left_from)

    grams = bundle_grams(loc, glo, wts)
    minus = [split(n) for n in minus_inverse([g[0] for g in grams])]
    fitted = [
        split(product(n, tuple(v[:, : 2 * BLK] for v in g[1]))) for n, g in zip(minus, grams)
    ]
    bundle_blocks(first, count, grams, fitted, t_in)
    away = jnp.where(right_home, 0, 1) + jnp.where(left_home, 0, 1)
    pl.semaphore_wait(barrier, 18 + away)

    def across_tc(i):
        return remote(t_in.at[1 - c, i], tc.at[i], s_tc.at[i], r_tc.at[i], pair)

    loop(0, 8, lambda i: across_tc(i).start())

    bundle_panel(first, count, grams, fitted, p_in)

    def panel_x(d):
        to = (x + d) % 4
        return remote(p_in.at[pl.ds(2 * to, 2)], px.at[d], s_px.at[d], r_px.at[d], at_x(to))

    loop(1, 4, lambda d: panel_x(d).start())

    def send_z1(d):
        to = (z + d) % 8
        return remote(ts.at[to, pl.ds(0, HALF)], tz1.at[d], s_z1.at[d], r_z1.at[d], at_z(to))

    def send_y1(d):
        to = (y + d) % 8
        return remote(ts.at[to, pl.ds(HALF, HALF)], ty1.at[d], s_y1.at[d], r_y1.at[d], at_y(to))

    def start_1(i):
        across_tc(i).wait_recv()
        ts[i] = (t_in[c, i].astype(F32) + tc[i].astype(F32)).astype(BF16)

        @pl.when(i != z)
        def _():
            send_z1((i + 8 - z) % 8).start()

        @pl.when(i != y)
        def _():
            send_y1((i + 8 - y) % 8).start()

    loop(0, 8, start_1)

    for d in range(1, 4):
        panel_x(d).wait_recv()
    for hh in range(2):
        total = p_in[2 * x + hh].astype(F32)
        for d in range(1, 4):
            total = total + px[d, hh].astype(F32)
        pa[hh] = total
    pp[...] = pa[1 - h].astype(BF16)
    copy_py = remote(pp, py, s_py, r_py, partner)
    copy_py.start()

    def wait_1(d):
        send_z1(d).wait_recv()
        send_y1(d).wait_recv()

    loop(1, 8, wait_1)
    sum_z = ts[z, 0:HALF].astype(F32)
    sum_y = ts[y, HALF:BLK].astype(F32)
    for d in range(1, 8):
        sum_z = sum_z + tz1[d].astype(F32)
        sum_y = sum_y + ty1[d].astype(F32)
    half2[0] = sum_z.astype(BF16)
    half2[1] = sum_y.astype(BF16)

    def send_y2(d):
        to = (y + d) % 8
        return remote(half2.at[0], ty2.at[d], s_y2.at[d], r_y2.at[d], at_y(to))

    def send_z2(d):
        to = (z + d) % 8
        return remote(half2.at[1], tz2.at[d], s_z2.at[d], r_z2.at[d], at_z(to))

    def start_2(d):
        send_y2(d).start()
        send_z2(d).start()

    loop(1, 8, start_2)

    copy_py.wait_recv()
    piece = (pa[h] + py[...].astype(F32)).astype(BF16)
    pc[...] = piece
    copy_rg = remote(pc, right.at[mine, right_j], s_rg, r_rg, right_to)
    copy_lg = remote(pc, left.at[c, mine], s_lg, r_lg, left_to)

    @pl.when(right_home)
    def _():
        right[mine, right_j] = piece

    @pl.when(jnp.logical_not(right_home))
    def _():
        copy_rg.start()

    @pl.when(left_home)
    def _():
        left[c, mine] = piece

    @pl.when(jnp.logical_not(left_home))
    def _():
        copy_lg.start()

    def wait_2(d):
        send_y2(d).wait_recv()
        send_z2(d).wait_recv()

    loop(1, 8, wait_2)
    sum_z = half2[0].astype(F32)
    sum_y = half2[1].astype(F32)
    for d in range(1, 8):
        sum_z = sum_z + ty2[d].astype(F32)
        sum_y = sum_y + tz2[d].astype(F32)
    half3[0] = sum_z.astype(BF16)
    half3[1] = sum_y.astype(BF16)

    def send_tx(d):
        return remote(half3, tx.at[d], s_tx.at[d], r_tx.at[d], at_x((x + d) % 4))

    loop(1, 4, lambda d: send_tx(d).start())
    loop(1, 4, lambda d: send_tx(d).wait_recv())
    sum_z, sum_y = half3[0].astype(F32), half3[1].astype(F32)
    for d in range(1, 4):
        sum_z = sum_z + tx[d, 0].astype(F32)
        sum_y = sum_y + tx[d, 1].astype(F32)
    t_out[c, z, 0:HALF] = sum_z
    t_out[c, y, HALF:BLK] = sum_y

    def upper(cc, i):
        return t_out.at[cc, i, pl.ds(0, HALF)]

    def lower(cc, i):
        return t_out.at[cc, i, pl.ds(HALF, HALF)]

    def send_z3(d):
        return remote(upper(c, z), upper(c, z), s_z3.at[d], r_z3.at[d], at_z((z + d) % 8))

    def send_y3(d):
        return remote(lower(c, y), lower(c, y), s_y3.at[d], r_y3.at[d], at_y((y + d) % 8))

    def got_z3(d):
        i = (z + 8 - d) % 8
        return remote(upper(c, i), upper(c, i), s_z3.at[d], r_z3.at[d], at_z(i))

    def got_y3(d):
        i = (y + 8 - d) % 8
        return remote(lower(c, i), lower(c, i), s_y3.at[d], r_y3.at[d], at_y(i))

    def across_z(cc, i):
        return remote(upper(cc, i), upper(cc, i), s_f.at[i], r_f.at[i], pair)

    def across_y(cc, i):
        return remote(lower(cc, i), lower(cc, i), s_f.at[8 + i], r_f.at[8 + i], pair)

    def start_3(d):
        send_z3(d).start()
        send_y3(d).start()

    loop(1, 8, start_3)
    across_z(c, z).start()
    across_y(c, y).start()

    def right_y(d):
        piece_at = right.at[mine, l]
        return remote(piece_at, piece_at, s_ry.at[d], r_ry.at[d], at_y((y + d) % 8))

    def got_right_y(d):
        i = (y + 8 - d) % 8
        piece_at = right.at[2 * x + i // 4, i % 4]
        return remote(piece_at, piece_at, s_ry.at[d], r_ry.at[d], at_y(i))

    def left_z(d):
        piece_at = left.at[c, z]
        return remote(piece_at, piece_at, s_lz.at[d], r_lz.at[d], at_z((z + d) % 8))

    def got_left_z(d):
        i = (z + 8 - d) % 8
        piece_at = left.at[c, i]
        return remote(piece_at, piece_at, s_lz.at[d], r_lz.at[d], at_z(i))

    @pl.when(jnp.logical_not(right_home))
    def _():
        remote(pc, right.at[mine, l], s_rg, r_rg, right_from).wait_recv()

    loop(1, 8, lambda d: right_y(d).start())

    @pl.when(jnp.logical_not(left_home))
    def _():
        remote(pc, left.at[c, z], s_lg, r_lg, left_from).wait_recv()

    loop(1, 8, lambda d: left_z(d).start())

    def arrived_3(d):
        got_z3(d).wait_recv()
        across_z(c, (z + 8 - d) % 8).start()
        got_y3(d).wait_recv()
        across_y(c, (y + 8 - d) % 8).start()

    loop(1, 8, arrived_3)

    def across(i):
        across_z(1 - c, i).wait_recv()
        across_y(1 - c, i).wait_recv()

    loop(0, 8, across)

    def right_x(hh, d):
        block = right.at[2 * x + hh]
        at = hh * 4 + d
        return remote(block, block, s_rx.at[at], r_rx.at[at], at_x((x + d) % 4))

    copy_lc = remote(left.at[c], left.at[c], s_lc, r_lc, pair)

    def pass_on():
        loop(1, 8, lambda d: got_right_y(d).wait_recv())
        for hh in range(2):
            loop(1, 4, lambda d: right_x(hh, d).start())
        loop(1, 8, lambda d: got_left_z(d).wait_recv())
        copy_lc.start()

    def panel_ready():
        remote(left.at[1 - c], left.at[1 - c], s_lc, r_lc, pair).wait_recv()
        for hh in range(2):

            def got_x(d):
                i = (x + 4 - d) % 4
                block = right.at[2 * i + hh]
                at = hh * 4 + d
                remote(block, block, s_rx.at[at], r_rx.at[at], at_x(i)).wait_recv()

            loop(1, 4, got_x)

    eliminate(t_out, left, right, out, pass_on, panel_ready)

    loop(0, 8, lambda i: across_tc(i).wait_send())
    copy_py.wait_send()
    copy_lc.wait_send()

    @pl.when(jnp.logical_not(right_home))
    def _():
        copy_rg.wait_send()

    @pl.when(jnp.logical_not(left_home))
    def _():
        copy_lg.wait_send()

    def sent_7(d):
        send_z1(d).wait_send()
        send_y1(d).wait_send()
        send_z2(d).wait_send()
        send_y2(d).wait_send()
        send_z3(d).wait_send()
        send_y3(d).wait_send()

    loop(1, 8, sent_7)

    def sent_3(d):
        panel_x(d).wait_send()
        send_tx(d).wait_send()
        right_x(0, d).wait_send()
        right_x(1, d).wait_send()

    loop(1, 4, sent_3)

    def sent_8(i):
        across_z(c, i).wait_send()
        across_y(c, i).wait_send()

    loop(0, 8, sent_8)

    def sent_panel(d):
        right_y(d).wait_send()
        left_z(d).wait_send()

    loop(1, 8, sent_panel)


def body(local_derivs, global_derivs, weights, first_block, bundle_count, trailing_block):
    vmem = pl.BlockSpec(memory_space=pltpu.VMEM)
    smem = pl.BlockSpec(memory_space=pltpu.SMEM)
    block = (BLK, BLK)
    shape = jax.ShapeDtypeStruct
    dma = pltpu.SemaphoreType.DMA
    half = (HALF, BLK)
    sems = (
        [dma((8,))] * 10
        + [dma((4,))] * 2
        + [dma((8,))] * 4
        + [dma((16,))] * 2
        + [dma((4,))] * 2
        + [dma, dma]
        + [dma, dma, dma, dma]
        + [dma((8,))] * 6
        + [dma, dma]
    )
    delta = pl.pallas_call(
        main_kernel,
        name="normal",
        in_specs=[smem, smem, vmem, vmem, vmem],
        out_specs=vmem,
        out_shape=shape(trailing_block.shape, F32),
        scratch_shapes=[
            pltpu.VMEM((2, PBLK) + block, BF16),
            pltpu.VMEM((PBLK,) + block, BF16),
            pltpu.VMEM((2, PBLK) + block, F32),
            pltpu.VMEM((2, PBLK) + block, BF16),
            pltpu.VMEM((PBLK, 4) + block, BF16),
            pltpu.VMEM((PBLK,) + block, BF16),
            pltpu.VMEM((PBLK,) + block, BF16),
            pltpu.VMEM((8,) + half, BF16),
            pltpu.VMEM((8,) + half, BF16),
            pltpu.VMEM((8,) + half, BF16),
            pltpu.VMEM((8,) + half, BF16),
            pltpu.VMEM((4, 2) + half, BF16),
            pltpu.VMEM((2,) + half, BF16),
            pltpu.VMEM((2,) + half, BF16),
            pltpu.VMEM((4, 2) + block, BF16),
            pltpu.VMEM((2,) + block, F32),
            pltpu.VMEM(block, BF16),
            pltpu.VMEM(block, BF16),
            pltpu.VMEM(block, BF16),
        ]
        + sems,
        compiler_params=pltpu.CompilerParams(collective_id=0, has_side_effects=True),
    )(first_block, bundle_count, local_derivs, global_derivs, weights)
    return trailing_block + delta


def solution(mesh):
    return jax.shard_map(
        body,
        mesh=mesh,
        in_specs=(
            P(("rec", "row", "col"), None, None),
            P(("rec", "row", "col"), None, None),
            P(("rec", "row", "col"), None),
            P(("rec", "row", "col")),
            P(("rec", "row", "col")),
            P(("rec", "row"), "col"),
        ),
        out_specs=P(("rec", "row"), "col"),
        check_vma=False,
    )
```
